32 devices in a mesh: groups: 2 (over y), gx: 4 (over z), gy: 2 (over x), sa: 2 (over core).
Axes of the slice: x: 2, y: 2, z: 4, core: 2. Of those that a mesh axis runs over, the one named last changes fastest.
Arguments:
- source_now: float32 [4, 128, 48, 128], P(('groups', 'sa'), 'gx', 'gy'), parts along dimension 0, may hold values from -6 to 6
- source_later: float32 [4, 128, 48, 128], P(('groups', 'sa'), 'gx', 'gy'), parts along dimension 0, may hold values from -6 to 6
- receiver_now: float32 [4, 128, 48, 128], P(('groups', 'sa'), 'gx', 'gy'), parts along dimension 0, may hold values from -6 to 6
- receiver_later: float32 [4, 128, 48, 128], P(('groups', 'sa'), 'gx', 'gy'), parts along dimension 0, may hold values from -6 to 6
- courant: float32 [128, 48, 128], P('gx', 'gy'), may hold values from 0.05 to 0.19
- wavelet: float32 [4, 12], P(('groups', 'sa')), parts along dimension 0, may hold values from -8 to 8
- traces: float32 [4, 12, 64], P(('groups', 'sa')), parts along dimension 0, may hold values from -6 to 6
- source_inline: int32 [4], P(('groups', 'sa')), parts along dimension 0, may hold values from 0 to 127
- source_crossline: int32 [4], P(('groups', 'sa')), parts along dimension 0, may hold values from 0 to 47
- receiver_inline: int32 [4, 64], P(('groups', 'sa')), parts along dimension 0, may hold values from 0 to 127
- receiver_crossline: int32 [4, 64], P(('groups', 'sa')), parts along dimension 0, may hold values from 0 to 47
Outputs:
- source_first: float32 [4, 128, 48, 128], P(('groups', 'sa'), 'gx', 'gy'), parts along dimension 0
- source_second: float32 [4, 128, 48, 128], P(('groups', 'sa'), 'gx', 'gy'), parts along dimension 0
- receiver_first: float32 [4, 128, 48, 128], P(('groups', 'sa'), 'gx', 'gy'), parts along dimension 0
- receiver_second: float32 [4, 128, 48, 128], P(('groups', 'sa'), 'gx', 'gy'), parts along dimension 0
- image_stack: float32 [256, 48, 128], P(('groups', 'gx', 'sa'), 'gy'), parts along dimension 0
The draws below stay inside these ranges and needn't reach their ends.
There are 2 independent parts, one for each index of `groups`. The reference program is written for one: setup_inputs(seed, part) draws one part's arguments, and reference() takes and returns one part's arrays. A program takes and returns all parts, laid end to end along the dimension named above; an argument that names none is the same for every part. Nothing has to cross between parts.
All inputs are finite; a program needn't handle non-finite values.
Results may differ from the reference program's by a relative error of at most 0.0003.
Values sent between devices are 32-bit elements; how exact they have to be, the bound alone decides.
No kernel may reach another device: no remote copies, remote signals or barrier semaphores. Data moves between devices by JAX's collectives and lax.ppermute only.
A program may use at most 128 MiB of HBM per device.

```python
import jax
import jax.numpy as jnp

SRC_DEPTH = 3
REC_DEPTH = 2
STEPS = 12
NX = 128
NY = 48
NZ = 128
SHOTS = 2
NREC = 64


def with_ends(drawn, key, low, high):
    extent = drawn.shape
    index_at = [jax.random.randint(jax.random.fold_in(key, axis), (), 0, extent[axis]) for axis in range(len(extent))]
    drawn = drawn.at[tuple(index_at)].set(low)
    longest = extent.index(max(extent))
    index_at[longest] = (index_at[longest] + 1) % extent[longest]
    return drawn.at[tuple(index_at)].set(high)


def block_levels(stream_key, extent, split, least, high):
    factor_of, own = 1.0, jax.random.fold_in(stream_key, 6)
    for position, blocks in split:
        draws = jnp.exp(jax.random.uniform(jax.random.fold_in(own, position), (blocks,), jnp.float32, least / len(split), high / len(split)))
        factor_of = factor_of * jnp.repeat(draws, extent[position] // blocks).reshape([-1 if axis == position else 1 for axis in range(len(extent))])
    return factor_of


def noise(own_key, dims, spread, bound, pieces=(), held_as=jnp.bfloat16):
    result = jax.random.normal(own_key, dims, jnp.float32) * spread
    if len(pieces) > 0:
        result = block_levels(own_key, dims, pieces, -0.22, 0.18) * result
    return jnp.clip(result, min=-bound, max=bound).astype(held_as)


def setup_inputs(seed: int = 0, part: int = 0) -> dict:
    key_list = jax.random.split(jax.random.key(seed), 12)
    part_keys = jax.random.split(jax.random.fold_in(key_list[11], part), 12)
    return {
        "source_now": noise(part_keys[0], (SHOTS, NX, NY, NZ), 1.0, 6.0, ((0, 2), (1, 4), (2, 2)), jnp.float32),
        "source_later": noise(part_keys[1], (SHOTS, NX, NY, NZ), 1.0, 6.0, ((0, 2), (1, 4), (2, 2)), jnp.float32),
        "receiver_now": noise(part_keys[2], (SHOTS, NX, NY, NZ), 1.0, 6.0, ((0, 2), (1, 4), (2, 2)), jnp.float32),
        "receiver_later": noise(part_keys[3], (SHOTS, NX, NY, NZ), 1.0, 6.0, ((0, 2), (1, 4), (2, 2)), jnp.float32),
        "courant": jnp.clip(0.05 + 0.14 * jax.random.uniform(key_list[4], (NX, NY, NZ), jnp.float32) ** block_levels(key_list[4], (NX, NY, NZ), ((0, 4), (1, 2)), -0.2, 0.2), 0.05, 0.19),
        "wavelet": noise(part_keys[5], (SHOTS, STEPS), 2.0, 8.0, ((0, 2),), jnp.float32),
        "traces": noise(part_keys[6], (SHOTS, STEPS, NREC), 1.0, 6.0, ((0, 2),), jnp.float32),
        "source_inline": jax.random.randint(part_keys[7], (SHOTS,), 0, NX).astype(jnp.int32),
        "source_crossline": jax.random.randint(part_keys[8], (SHOTS,), 0, NY).astype(jnp.int32),
        "receiver_inline": with_ends(jax.random.randint(part_keys[9], (SHOTS, NREC), 0, NX), jax.random.fold_in(part_keys[9], 1), 0, NX - 1).astype(jnp.int32),
        "receiver_crossline": with_ends(jax.random.randint(part_keys[10], (SHOTS, NREC), 0, NY), jax.random.fold_in(part_keys[10], 1), 0, NY - 1).astype(jnp.int32),
    }


COEFFS = (-205.0 / 72.0, 8.0 / 5.0, -1.0 / 5.0, 8.0 / 315.0, -1.0 / 560.0)


def laplace(padded):
    inline_span = padded.shape[0] - 8
    cross_span = padded.shape[1] - 8
    center = padded[4:4 + inline_span, 4:4 + cross_span]
    depth_span = center.shape[2]
    depth_padded = jnp.pad(center, ((0, 0), (0, 0), (4, 4)))
    summed = (3.0 * COEFFS[0]) * center
    for distance in range(1, 5):
        neighbours = padded[4 + distance:4 + distance + inline_span, 4:4 + cross_span] + padded[4 - distance:4 - distance + inline_span, 4:4 + cross_span]
        neighbours = neighbours + padded[4:4 + inline_span, 4 + distance:4 + distance + cross_span] + padded[4:4 + inline_span, 4 - distance:4 - distance + cross_span]
        neighbours = neighbours + depth_padded[:, :, 4 + distance:4 + distance + depth_span] + depth_padded[:, :, 4 - distance:4 - distance + depth_span]
        summed = summed + COEFFS[distance] * neighbours
    return summed


def reference(source_now, source_later, receiver_now, receiver_later, courant, wavelet, traces, source_inline, source_crossline, receiver_inline, receiver_crossline):
    depth_axis = jnp.arange(NZ)
    source_layer = (depth_axis == SRC_DEPTH).astype(jnp.float32)
    receiver_layer = (depth_axis == REC_DEPTH).astype(jnp.float32)
    widths = ((4, 4), (4, 4), (0, 0))
    firsts_source, seconds_source, firsts_receiver, seconds_receiver = [], [], [], []
    image_total = jnp.zeros((NX, NY, NZ), jnp.float32)
    for shot_index in range(SHOTS):
        source_field = source_now[shot_index]
        source_prior = source_later[shot_index]
        receiver_field = receiver_now[shot_index]
        receiver_prior = receiver_later[shot_index]
        source_spot = jnp.zeros((NX, NY), jnp.float32).at[source_inline[shot_index], source_crossline[shot_index]].set(1.0)
        record_planes = jnp.zeros((STEPS, NX, NY), jnp.float32).at[:, receiver_inline[shot_index], receiver_crossline[shot_index]].add(traces[shot_index])
        correlation = jnp.zeros((NX, NY, NZ), jnp.float32)
        for moment in range(STEPS):
            source_curve = laplace(jnp.pad(source_field, widths))
            source_new = 2.0 * source_field - source_prior + courant * (source_curve + (wavelet[shot_index, moment] * source_spot)[:, :, None] * source_layer)
            receiver_curve = laplace(jnp.pad(receiver_field, widths))
            receiver_new = 2.0 * receiver_field - receiver_prior + courant * (receiver_curve + record_planes[moment][:, :, None] * receiver_layer)
            correlation = correlation + source_new * receiver_new
            source_prior, source_field = source_field, source_new
            receiver_prior, receiver_field = receiver_field, receiver_new
        firsts_source.append(source_field)
        seconds_source.append(source_prior)
        firsts_receiver.append(receiver_field)
        seconds_receiver.append(receiver_prior)
        image_total = image_total + correlation
    image_stack = image_total / STEPS
    return (jnp.stack(firsts_source), jnp.stack(seconds_source), jnp.stack(firsts_receiver), jnp.stack(seconds_receiver), image_stack)
```

```python
import itertools

import jax
import jax.numpy as jnp
from jax import lax
from jax.experimental import pallas as pl
from jax.experimental.pallas import tpu as pltpu
from jax.sharding import PartitionSpec as P

SRC_DEPTH = 3
REC_DEPTH = 2
STEPS = 12
COEFFS = (-205.0 / 72.0, 8.0 / 5.0, -1.0 / 5.0, 8.0 / 315.0, -1.0 / 560.0)
RADIUS = 4
LANES = 128
SUB = 8
DEEP = 2
HALO = RADIUS * DEEP
CHUNK = 8
GENERAL_BLOCK = 4
GENERAL_BLOCKS = 3
VMEM_LIMIT = 24 << 20

VM = pl.BlockSpec(memory_space=pltpu.VMEM)
SM = pl.BlockSpec(memory_space=pltpu.SMEM)
ANY = pl.BlockSpec(memory_space=pl.ANY)
F32 = jnp.float32


class Geometry:
    def __init__(self, mesh, nx, ny):
        self.mesh = mesh
        self.nx, self.ny = nx, ny
        self.xe = nx + 2 * HALO
        self.win = ny + HALO
        self.jn = self.win // SUB
        self.gx = mesh.shape["gx"]
        self.srows = ny // self.jn

    def place(self):
        p = lax.axis_index("gy")
        g = lax.axis_index("gx")
        odd = g % 2
        even_right = odd == 0
        even_ok = jnp.logical_or(odd == 1, g + 1 < self.gx)
        odd_right = odd == 1
        odd_ok = jnp.logical_or(jnp.logical_and(odd == 1, g + 1 < self.gx), jnp.logical_and(odd == 0, g > 0))
        return p, g, ((even_right, even_ok), (odd_right, odd_ok))


def permutation(mesh, move):
    names = mesh.axis_names
    sizes = [mesh.shape[n] for n in names]
    pairs = []
    for idx in itertools.product(*[range(s) for s in sizes]):
        at = dict(zip(names, idx))
        to = move(dict(at))
        if to is None:
            to = dict(at)
            to["sa"] = (mesh.shape["sa"] - 1) - at["sa"]
        a = b = 0
        for n, s in zip(names, sizes):
            a, b = a * s + at[n], b * s + to[n]
        pairs.append((a, b))
    return pairs


def neighbour(mesh, parity, flip_y, step_x):
    count = mesh.shape["gx"]

    def move(at):
        if step_x:
            to = at["gx"] + 1 if at["gx"] % 2 == parity else at["gx"] - 1
            if to < 0 or to >= count:
                return None
            at["gx"] = to
        if flip_y:
            at["gy"] = 1 - at["gy"]
        return at

    return permutation(mesh, move)


def call(body, out_shapes, specs, args, out_specs=None, scratch=(), aliases=None):
    return pl.pallas_call(
        body,
        out_shape=out_shapes,
        in_specs=specs,
        out_specs=out_specs if out_specs is not None else [VM] * len(out_shapes),
        scratch_shapes=list(scratch),
        input_output_aliases=aliases or {},
        compiler_params=pltpu.CompilerParams(vmem_limit_bytes=VMEM_LIMIT),
    )(*args)


def shape(*dims):
    return jax.ShapeDtypeStruct(dims, F32)


def message_shapes(geo, first):
    extra = 3 if first else 0
    y = shape(2 * geo.nx + extra * geo.nx // 2, SUB, LANES)
    x = shape(2 * HALO + extra * RADIUS, geo.ny, LANES)
    d = shape(2 * RADIUS // 2, SUB, LANES)
    return [y, x, x, d, d]


def pack(geo, fields, extras, messages):
    p, _, sides = geo.place()
    my, me, mo, de, do = messages
    nx = geo.nx

    def ybody(x, carry):
        for f, u in enumerate(fields):
            for i in range(2):
                my[f * nx + x, 4 * i : 4 * i + 4, :] = u[x + HALO, pl.ds(4 + i - 2 * p, 4, stride=SUB), :]
        return carry

    lax.fori_loop(0, nx, ybody, 0, unroll=4)
    if extras:

        def yextra(h, carry):
            for f, u in enumerate(extras):
                for i in range(2):
                    rows = u[2 * h + i + HALO, pl.ds(5 - 3 * p, 4, stride=SUB), :]
                    my[2 * nx + f * (nx // 2) + h, 4 * i : 4 * i + 4, :] = rows
            return carry

        lax.fori_loop(0, nx // 2, yextra, 0, unroll=2)
    for (right, _), mx, md in zip(sides, (me, mo), (de, do)):
        wide = jnp.where(right, nx, HALO)
        thin = jnp.where(right, nx + HALO - RADIUS, HALO)

        def xbody(i, carry, mx=mx, wide=wide):
            for f, u in enumerate(fields):
                for q in range(geo.srows):
                    mx[f * HALO + i, 4 * q : 4 * q + 4, :] = u[wide + i, pl.ds(2 * p + q, 4, stride=SUB), :]
            return carry

        lax.fori_loop(0, HALO, xbody, 0, unroll=2)
        for i in range(RADIUS):
            for f, u in enumerate(extras):
                for q in range(geo.srows):
                    mx[2 * HALO + f * RADIUS + i, 4 * q : 4 * q + 4, :] = u[thin + i, pl.ds(2 * p + q, 4, stride=SUB), :]
            for f, u in enumerate(fields):
                rows = u[thin + i, pl.ds(5 - 3 * p, 4, stride=SUB), :]
                md[2 * f + i // 2, 4 * (i % 2) : 4 * (i % 2) + 4, :] = rows


def unpack(geo, fields, extras, messages):
    p, _, sides = geo.place()
    my, me, mo, de, do = messages
    nx = geo.nx

    def ybody(x, carry):
        for f, u in enumerate(fields):
            for i in range(2):
                u[x + HALO, pl.ds(6 + i - 6 * p, 4, stride=SUB), :] = my[f * nx + x, 4 * i : 4 * i + 4, :]
        return carry

    lax.fori_loop(0, nx, ybody, 0, unroll=4)
    if extras:

        def yextra(h, carry):
            for f, u in enumerate(extras):
                for i in range(2):
                    rows = my[2 * nx + f * (nx // 2) + h, 4 * i : 4 * i + 4, :]
                    u[2 * h + i + HALO, pl.ds(6 - 5 * p, 4, stride=SUB), :] = rows
            return carry

        lax.fori_loop(0, nx // 2, yextra, 0, unroll=2)
    for (right, ok), mx, md in zip(sides, (me, mo), (de, do)):

        @pl.when(ok)
        def _(right=right, mx=mx, md=md):
            wide = jnp.where(right, nx + HALO, 0)
            thin = jnp.where(right, nx + HALO, HALO - RADIUS)

            def xbody(i, carry):
                for f, u in enumerate(fields):
                    for q in range(geo.srows):
                        u[wide + i, pl.ds(2 * p + q, 4, stride=SUB), :] = mx[f * HALO + i, 4 * q : 4 * q + 4, :]
                return carry

            lax.fori_loop(0, HALO, xbody, 0, unroll=2)
            for i in range(RADIUS):
                for f, u in enumerate(extras):
                    for q in range(geo.srows):
                        rows = mx[2 * HALO + f * RADIUS + i, 4 * q : 4 * q + 4, :]
                        u[thin + i, pl.ds(2 * p + q, 4, stride=SUB), :] = rows
                for f, u in enumerate(fields):
                    rows = md[2 * f + i // 2, 4 * (i % 2) : 4 * (i % 2) + 4, :]
                    u[thin + i, pl.ds(6 - 5 * p, 4, stride=SUB), :] = rows


def load_kernel(geo):
    nx, ny, xe = geo.nx, geo.ny, geo.xe

    def body(s0, s1, r0, r1, c0, us, ur, ps, pr, cc, dw, my, me, mo, de, do, pad, sem):
        p, _, _ = geo.place()
        inside = pl.ds(pl.multiple_of(SUB * p, SUB), ny)
        sources = (s0.at[0], r0.at[0], s1.at[0], r1.at[0], c0)
        copies = [
            pltpu.make_async_copy(src, pad.at[f, :, inside, :], sem.at[f]) for f, src in enumerate(sources)
        ]
        for copy in copies:
            copy.start()
        outside = pl.ds(pl.multiple_of(ny - ny * p, SUB), SUB)
        targets = (us, ur, ps, pr, cc)
        row = lax.broadcasted_iota(jnp.int32, (LANES, LANES), 0)
        col = lax.broadcasted_iota(jnp.int32, (LANES, LANES), 1)
        gap = jnp.abs(row - col)
        d = jnp.zeros((LANES, LANES), F32)
        for k in range(1, RADIUS + 1):
            d = jnp.where(gap == k, COEFFS[k], d)
        hi = d.astype(jnp.bfloat16)
        lo = (d - hi.astype(F32)).astype(jnp.bfloat16)
        dw[0:LANES, 0:LANES] = hi
        dw[0:LANES, LANES : 2 * LANES] = lo
        dw[LANES : 2 * LANES, 0:LANES] = hi
        dw[LANES : 2 * LANES, LANES : 2 * LANES] = jnp.zeros_like(lo)
        zero = jnp.zeros((geo.win, LANES), F32)
        for f, u in enumerate(targets):
            for x in range(nx):
                pad[f, x, outside, :] = jnp.zeros((SUB, LANES), F32)
            for x in range(HALO):
                u[x] = zero
                u[nx + HALO + x] = zero
        for f, (u, copy) in enumerate(zip(targets, copies)):
            copy.wait()

            def turn(x, carry, f=f, u=u):
                for j in range(geo.jn):
                    u[x + HALO, SUB * j : SUB * j + SUB, :] = pad[f, x, pl.ds(j, SUB, stride=geo.jn), :]
                return carry

            lax.fori_loop(0, nx, turn, 0, unroll=4)
        pack(geo, (us, ur), (ps, pr, cc), (my, me, mo, de, do))

    return body


def receiver_kernel(geo, nrec):
    rows_all = geo.xe * geo.win
    block = 128

    def body(ri, rc, traces, out, table):
        p, g, _ = geo.place()
        x = ri[...] - g * geo.nx + HALO
        w = rc[...] - p * geo.ny + SUB * p
        ok = (x >= 0) & (x < geo.xe) & (w >= 0) & (w < geo.win)
        shift = geo.jn.bit_length() - 1
        row = x * geo.win + (w & (geo.jn - 1)) * SUB + (w >> shift)
        row = jnp.where(ok, row, -1)
        table[...] = jnp.zeros_like(table)
        table[0:STEPS, :] = traces[0]
        tab = table[...]

        def chunk(i, carry):
            at = i * block + lax.broadcasted_iota(jnp.int32, (block, nrec), 0)
            hot = jnp.where(at == row, 1.0, 0.0).astype(F32)
            plane = lax.dot_general(
                hot, tab, (((1,), (1,)), ((), ())), precision=lax.Precision.HIGHEST, preferred_element_type=F32
            )
            planes = block // geo.win
            out[pl.ds(i * planes, planes)] = plane.reshape(planes, geo.win, LANES)
            return carry

        lax.fori_loop(0, rows_all // block, chunk, 0)

    return body


def depth_part(geo, u, z, dw, first, count):
    w = dw[...]

    def chunk(i, carry):
        at = first + i * CHUNK
        rows = u[pl.ds(at, CHUNK)].reshape(CHUNK * geo.win, LANES)
        hi = rows.astype(jnp.bfloat16)
        lo = (rows - hi.astype(F32)).astype(jnp.bfloat16)
        both = jnp.dot(jnp.concatenate([hi, lo], axis=1), w, preferred_element_type=F32)
        z[pl.ds(at, CHUNK)] = (both[:, :LANES] + both[:, LANES:]).reshape(CHUNK, geo.win, LANES)
        return carry

    lax.fori_loop(0, count // CHUNK, chunk, 0)


def update_plane(geo, u, prior, cc, z, x, sub, extra):
    jn = geo.jn
    mid = [u[x, SUB * j : SUB * j + SUB, :] for j in range(jn)]
    first, last = sub == 0, sub == SUB - 1
    below = [jnp.where(first, 0.0, pltpu.roll(v, 1, 0)) for v in mid]
    above = [jnp.where(last, 0.0, pltpu.roll(v, SUB - 1, 0)) for v in mid]
    line = below + mid + above
    news = []
    for j in range(jn):
        tile = slice(SUB * j, SUB * j + SUB)
        acc = z[x, tile, :] + (3.0 * COEFFS[0]) * mid[j]
        for k in range(1, RADIUS + 1):
            near = (u[x + k, tile, :] + u[x - k, tile, :]) + (line[jn + j + k] + line[jn + j - k])
            acc = acc + COEFFS[k] * near
        if extra is not None:
            acc = acc + extra(j)
        new = (2.0 * mid[j] - prior[x, tile, :]) + cc[x, tile, :] * acc
        prior[x, tile, :] = new
        news.append(new)
    return news


def one_step(geo, moment, us, ur, ps, pr, cc, gg, corr, zs, zr, dw, wavelet, src, first, count, fresh):
    nx = geo.nx
    depth_part(geo, us, zs, dw, first, count)
    depth_part(geo, ur, zr, dw, first, count)
    sub = lax.broadcasted_iota(jnp.int32, (SUB, LANES), 0)
    lane = lax.broadcasted_iota(jnp.int32, (SUB, LANES), 1)
    at_depth = lane == REC_DEPTH

    def plane(x, carry, inner):
        def fed(j):
            rows = gg[x, SUB * j : SUB * j + SUB, :]
            return jnp.where(at_depth, pltpu.roll(rows, (REC_DEPTH - moment) % LANES, 1), 0.0)

        news = update_plane(geo, us, ps, cc, zs, x, sub, None)
        newr = update_plane(geo, ur, pr, cc, zr, x, sub, fed)
        if inner:
            for j in range(geo.jn):
                tile = slice(SUB * j, SUB * j + SUB)
                product = news[j] * newr[j]
                if not fresh:
                    product = product + corr[x - HALO, tile, :]
                corr[x - HALO, tile, :] = product
        return carry

    edge = HALO - first
    if edge > 0:
        lax.fori_loop(first, HALO, lambda x, c: plane(x, c, False), 0)
        lax.fori_loop(nx + HALO, first + count, lambda x, c: plane(x, c, False), 0)
    lax.fori_loop(HALO, nx + HALO, lambda x, c: plane(x, c, True), 0)
    xs, row, ok = src

    @pl.when(ok & (xs >= first) & (xs < first + count))
    def _():
        shot = jnp.where(lane[0:1] == SRC_DEPTH, wavelet[0, moment], 0.0)
        add = cc[xs, pl.ds(row, 1), :] * shot
        ps[xs, pl.ds(row, 1), :] = ps[xs, pl.ds(row, 1), :] + add

        @pl.when((xs >= HALO) & (xs < nx + HALO))
        def _():
            corr[xs - HALO, pl.ds(row, 1), :] = (
                corr[xs - HALO, pl.ds(row, 1), :] + add * pr[xs, pl.ds(row, 1), :]
            )


def round_kernel(geo, block, last):
    first_round = block == 0

    def body(*refs):
        refs = list(refs)
        take = lambda n: [refs.pop(0) for _ in range(n)]
        us0, ur0, ps0, pr0, cc0, dw, gg = take(7)
        if not first_round:
            take(1)
        inputs = take(5)
        wavelet, sx, sy = take(3)
        us, ur, ps, pr, cc, corr = take(6)
        outs = [] if last else take(5)
        zs, zr = take(2)
        p, g, _ = geo.place()
        xs = sx[0] - g * geo.nx + HALO
        w = sy[0] - p * geo.ny + SUB * p
        ok = (w >= 0) & (w < geo.win) & (xs >= 0) & (xs < geo.xe)
        shift = geo.jn.bit_length() - 1
        src = (xs, (w & (geo.jn - 1)) * SUB + (w >> shift), ok)
        unpack(geo, (us, ur), (ps, pr, cc) if first_round else (), inputs)
        common = (cc, gg, corr, zs, zr, dw, wavelet, src)
        one_step(geo, DEEP * block, us, ur, ps, pr, *common, HALO - RADIUS, geo.nx + 2 * RADIUS, first_round)
        one_step(geo, DEEP * block + 1, ps, pr, us, ur, *common, HALO, geo.nx, False)
        if not last:
            pack(geo, (us, ur), (), outs)

    return body


def corr_kernel(geo, halves):
    part = geo.nx // halves

    def body(corr, mine, other, pad):
        p, _, _ = geo.place()
        q = lax.axis_index("sa")

        def turn(x, carry):
            for j in range(geo.jn):
                pad[x, pl.ds(j, SUB, stride=geo.jn), :] = corr[x, SUB * j : SUB * j + SUB, :]
            return carry

        lax.fori_loop(0, geo.nx, turn, 0, unroll=4)
        inside = pl.ds(pl.multiple_of(SUB * p, SUB), geo.ny)

        def split(x, carry):
            mine[x] = pad[q * part + x, inside, :]
            other[x] = pad[(halves - 1 - q) * part + x, inside, :]
            return carry

        lax.fori_loop(0, part, split, 0, unroll=2)

    return body


def store_kernel(geo):
    def body(us, ur, ps, pr, o0, o1, o2, o3, pad, sem):
        p, _, _ = geo.place()
        inside = pl.ds(pl.multiple_of(SUB * p, SUB), geo.ny)
        copies = []
        for f, (u, o) in enumerate(((us, o0), (ps, o1), (ur, o2), (pr, o3))):

            def turn(x, carry, f=f, u=u):
                for j in range(geo.jn):
                    pad[f, x, pl.ds(j, SUB, stride=geo.jn), :] = u[x + HALO, SUB * j : SUB * j + SUB, :]
                return carry

            lax.fori_loop(0, geo.nx, turn, 0, unroll=4)
            copy = pltpu.make_async_copy(pad.at[f, :, inside, :], o.at[0], sem.at[f])
            copy.start()
            copies.append(copy)
        for copy in copies:
            copy.wait()

    return body


def fast_body(mesh):
    def run(sn, sl, rn, rl, courant, wavelet, traces, si, sc, ri, rc):
        nx, ny, nz = courant.shape
        geo = Geometry(mesh, nx, ny)
        state = shape(geo.xe, geo.win, nz)
        names = mesh.axis_names
        routes = [
            neighbour(mesh, 0, True, False),
            neighbour(mesh, 0, False, True),
            neighbour(mesh, 1, False, True),
            neighbour(mesh, 0, True, True),
            neighbour(mesh, 1, True, True),
        ]
        send = lambda ms: [lax.ppermute(m, names, route) for m, route in zip(ms, routes)]
        loaded = call(
            load_kernel(geo),
            [state] * 5
            + [jax.ShapeDtypeStruct((2 * LANES, 2 * LANES), jnp.bfloat16)]
            + message_shapes(geo, True),
            [ANY] * 5,
            (sn, sl, rn, rl, courant),
            scratch=[pltpu.VMEM((5, nx, geo.win, nz), F32), pltpu.SemaphoreType.DMA((5,))],
        )
        us, ur, ps, pr, cc, dw = loaded[:6]
        messages = send(loaded[6:])
        nrec = traces.shape[2]
        (gg,) = call(
            receiver_kernel(geo, nrec),
            [state],
            [VM] * 3,
            (ri, rc, traces),
            scratch=[pltpu.VMEM((LANES, nrec), F32)],
        )
        corr = None
        blocks = STEPS // DEEP
        for block in range(blocks):
            last = block == blocks - 1
            args = [us, ur, ps, pr, cc, dw, gg] + ([] if corr is None else [corr]) + messages
            specs = [VM] * len(args) + [SM] * 3
            aliases = {i: i for i in range(5)}
            if corr is not None:
                aliases[7] = 5
            outs = call(
                round_kernel(geo, block, last),
                [state] * 5 + [shape(nx, geo.win, nz)] + ([] if last else message_shapes(geo, False)),
                specs,
                args + [wavelet, si, sc],
                scratch=[pltpu.VMEM((geo.xe, geo.win, nz), F32)] * 2,
                aliases=aliases,
            )
            us, ur, ps, pr, cc, corr = outs[:6]
            if not last:
                messages = send(outs[6:])
        halves = mesh.shape["sa"]
        part = shape(nx // halves, ny, nz)
        mine, other = call(
            corr_kernel(geo, halves), [part] * 2, [VM], (corr,), scratch=[pltpu.VMEM((nx, geo.win, nz), F32)]
        )
        pairs = [(i, halves - 1 - i) for i in range(halves)]
        image = (mine + lax.ppermute(other, "sa", pairs)) / STEPS
        fields = call(
            store_kernel(geo),
            [shape(1, nx, ny, nz)] * 4,
            [VM] * 4,
            (us, ur, ps, pr),
            out_specs=[ANY] * 4,
            scratch=[pltpu.VMEM((4, nx, geo.win, nz), F32), pltpu.SemaphoreType.DMA((4,))],
        )
        return (*fields, image)

    return run


def padded_2(cells, sides, width):
    for axis, dim in sides:
        count = lax.axis_size(axis)
        ends = count - 1
        head = lax.slice_in_dim(cells, 0, width, axis=dim)
        tail = lax.slice_in_dim(cells, cells.shape[dim] - width, cells.shape[dim], axis=dim)
        cells = jnp.concatenate(
            [
                lax.ppermute(tail, axis, [(i, (i + 1) % count) for i in range(ends)]),
                cells,
                lax.ppermute(head, axis, [((i + 1) % count, i) for i in range(ends)]),
            ],
            axis=dim,
        )
    return cells


def laplace(padded):
    inline_span = padded.shape[0] - 8
    cross_span = padded.shape[1] - 8
    center = padded[4 : 4 + inline_span, 4 : 4 + cross_span]
    depth_span = center.shape[2]
    depth_padded = jnp.pad(center, ((0, 0), (0, 0), (4, 4)))
    summed = 3.0 * COEFFS[0] * center
    for distance in range(1, 5):
        neighbours = (
            padded[4 + distance : 4 + distance + inline_span, 4 : 4 + cross_span]
            + padded[4 - distance : 4 - distance + inline_span, 4 : 4 + cross_span]
        )
        neighbours = (
            neighbours
            + padded[4 : 4 + inline_span, 4 + distance : 4 + distance + cross_span]
            + padded[4 : 4 + inline_span, 4 - distance : 4 - distance + cross_span]
        )
        neighbours = (
            neighbours
            + depth_padded[:, :, 4 + distance : 4 + distance + depth_span]
            + depth_padded[:, :, 4 - distance : 4 - distance + depth_span]
        )
        summed = summed + COEFFS[distance] * neighbours
    return summed


def crop_margin(values, margin_cut):
    if margin_cut == 0:
        return values
    return values[
        margin_cut : values.shape[0] - margin_cut, margin_cut : values.shape[1] - margin_cut
    ]


def general_body(
    source_now,
    source_later,
    receiver_now,
    receiver_later,
    courant,
    wavelet,
    traces,
    source_inline,
    source_crossline,
    receiver_inline,
    receiver_crossline,
):
    inline_count, cross_count, depth_count = courant.shape
    inline_anchor = lax.axis_index("gx") * inline_count
    cross_anchor = lax.axis_index("gy") * cross_count
    inline_extent = inline_count * lax.axis_size("gx")
    cross_extent = cross_count * lax.axis_size("gy")
    depth_axis = jnp.arange(depth_count)
    source_layer = (depth_axis == SRC_DEPTH).astype(jnp.float32)
    receiver_layer = (depth_axis == REC_DEPTH).astype(jnp.float32)
    wavelet_row = wavelet[0]
    records = traces[0]
    source_field = source_now[0]
    source_prior = source_later[0]
    receiver_field = receiver_now[0]
    receiver_prior = receiver_later[0]
    correlation = jnp.zeros(courant.shape, jnp.float32)
    widest = 4 * (GENERAL_BLOCK - 1)
    speed_wide = padded_2(courant, (("gx", 0), ("gy", 1)), widest)
    inline_cells = inline_anchor - widest + jnp.arange(inline_count + 2 * widest)
    cross_cells = cross_anchor - widest + jnp.arange(cross_count + 2 * widest)
    inline_hot = (inline_cells[:, None] == receiver_inline[0][None, :]).astype(jnp.float32)
    cross_hot = (receiver_crossline[0][:, None] == cross_cells[None, :]).astype(jnp.float32)
    receivers = cross_hot.shape[0]
    weighted = (records.T[:, :, None] * cross_hot[:, None, :]).reshape(
        receivers, STEPS * cross_hot.shape[1]
    )
    planes = jnp.dot(inline_hot, weighted, precision=lax.Precision.HIGHEST).reshape(
        inline_hot.shape[0], STEPS, cross_hot.shape[1]
    )
    source_spot = (inline_cells == source_inline[0]).astype(jnp.float32)[:, None] * (
        cross_cells == source_crossline[0]
    ).astype(jnp.float32)[None, :]
    inline_in = ((inline_cells >= 0) & (inline_cells < inline_extent)).astype(jnp.float32)
    cross_in = ((cross_cells >= 0) & (cross_cells < cross_extent)).astype(jnp.float32)
    inside = inline_in[:, None, None] * cross_in[None, :, None]
    planes, source_spot, inside = (planes, source_spot, inside)
    for segment in range(GENERAL_BLOCKS):
        source_wide, receiver_wide = (
            padded_2(source_field, (("gx", 0), ("gy", 1)), 4 * GENERAL_BLOCK),
            padded_2(receiver_field, (("gx", 0), ("gy", 1)), 4 * GENERAL_BLOCK),
        )
        source_back, receiver_back = (
            padded_2(source_prior, (("gx", 0), ("gy", 1)), widest),
            padded_2(receiver_prior, (("gx", 0), ("gy", 1)), widest),
        )
        for substep in range(GENERAL_BLOCK):
            margin = 4 * (GENERAL_BLOCK - 1 - substep)
            offset = widest - margin
            moment = segment * GENERAL_BLOCK + substep
            speed = crop_margin(speed_wide, offset)
            region = crop_margin(inside, offset)
            record_plane = crop_margin(planes[:, moment, :], offset)
            spot_plane = crop_margin(source_spot, offset)
            source_centre = crop_margin(source_wide, 4)
            receiver_centre = crop_margin(receiver_wide, 4)
            source_new = region * (
                2.0 * source_centre
                - source_back
                + speed
                * (
                    laplace(source_wide)
                    + (wavelet_row[moment] * spot_plane)[:, :, None] * source_layer
                )
            )
            receiver_new = region * (
                2.0 * receiver_centre
                - receiver_back
                + speed * (laplace(receiver_wide) + record_plane[:, :, None] * receiver_layer)
            )
            correlation = correlation + crop_margin(source_new, margin) * crop_margin(
                receiver_new, margin
            )
            source_wide, receiver_wide = (source_new, receiver_new)
            if margin > 0:
                source_back = crop_margin(source_centre, 4)
                receiver_back = crop_margin(receiver_centre, 4)
            else:
                source_back = source_centre
                receiver_back = receiver_centre
        source_field, source_prior = (source_wide, source_back)
        receiver_field, receiver_prior = (receiver_wide, receiver_back)
    image_part = lax.psum_scatter(correlation, "sa", scatter_dimension=0, tiled=True) / STEPS
    return (
        source_field[None],
        source_prior[None],
        receiver_field[None],
        receiver_prior[None],
        image_part,
    )


def any_body(mesh):
    fast = fast_body(mesh)

    def run(*args):
        nx, ny, nz = args[4].shape
        fits = mesh.shape["gy"] == 2 and mesh.shape["sa"] == 2 and nz == LANES
        fits = fits and (ny + HALO) == RADIUS * SUB and nx % (2 * CHUNK) == 0
        return (fast if fits else general_body)(*args)

    return run


def solution(mesh):
    in_specs = (
        P(("groups", "sa"), "gx", "gy", None),
        P(("groups", "sa"), "gx", "gy", None),
        P(("groups", "sa"), "gx", "gy", None),
        P(("groups", "sa"), "gx", "gy", None),
        P("gx", "gy", None),
        P(("groups", "sa"), None),
        P(("groups", "sa"), None, None),
        P(("groups", "sa")),
        P(("groups", "sa")),
        P(("groups", "sa"), None),
        P(("groups", "sa"), None),
    )
    out_specs = (
        P(("groups", "sa"), "gx", "gy", None),
        P(("groups", "sa"), "gx", "gy", None),
        P(("groups", "sa"), "gx", "gy", None),
        P(("groups", "sa"), "gx", "gy", None),
        P(("groups", "gx", "sa"), "gy", None),
    )
    return jax.shard_map(any_body(mesh), mesh=mesh, in_specs=in_specs, out_specs=out_specs, check_vma=False)
```

```python
import itertools

import jax
import jax.numpy as jnp
from jax import lax
from jax.experimental import pallas as pl
from jax.experimental.pallas import tpu as pltpu
from jax.sharding import PartitionSpec as P

SRC_DEPTH = 3
REC_DEPTH = 2
STEPS = 12
COEFFS = (-205.0 / 72.0, 8.0 / 5.0, -1.0 / 5.0, 8.0 / 315.0, -1.0 / 560.0)
RADIUS = 4
LANES = 128
SUB = 8
DEEP = 2
HALO = RADIUS * DEEP
GROUP = 8
RATIOS = [c / COEFFS[1] for c in COEFFS]
GENERAL_BLOCK = 4
GENERAL_BLOCKS = 3
VMEM_LIMIT = 24 << 20

VM = pl.BlockSpec(memory_space=pltpu.VMEM)
SM = pl.BlockSpec(memory_space=pltpu.SMEM)
HBM = pl.BlockSpec(memory_space=pltpu.HBM)
F32 = jnp.float32


class Geometry:
    def __init__(self, mesh, nx, ny):
        self.mesh = mesh
        self.nx, self.ny = nx, ny
        self.xe = nx + 2 * HALO
        self.win = ny + HALO
        self.jn = self.win // SUB
        self.gx = mesh.shape["gx"]
        self.srows = ny // self.jn

    def place(self):
        p = lax.axis_index("gy")
        g = lax.axis_index("gx")
        odd = g % 2
        even_right = odd == 0
        even_ok = jnp.logical_or(odd == 1, g + 1 < self.gx)
        odd_right = odd == 1
        odd_ok = jnp.logical_or(jnp.logical_and(odd == 1, g + 1 < self.gx), jnp.logical_and(odd == 0, g > 0))
        return p, g, ((even_right, even_ok), (odd_right, odd_ok))


def permutation(mesh, move):
    names = mesh.axis_names
    sizes = [mesh.shape[n] for n in names]
    pairs = []
    for idx in itertools.product(*[range(s) for s in sizes]):
        at = dict(zip(names, idx))
        to = move(dict(at))
        if to is None:
            to = dict(at)
            to["sa"] = (mesh.shape["sa"] - 1) - at["sa"]
        a = b = 0
        for n, s in zip(names, sizes):
            a, b = a * s + at[n], b * s + to[n]
        pairs.append((a, b))
    return pairs


def neighbour(mesh, parity, flip_y, step_x):
    count = mesh.shape["gx"]

    def move(at):
        if step_x:
            to = at["gx"] + 1 if at["gx"] % 2 == parity else at["gx"] - 1
            if to < 0 or to >= count:
                return None
            at["gx"] = to
        if flip_y:
            at["gy"] = 1 - at["gy"]
        return at

    return permutation(mesh, move)


def call(body, out_shapes, specs, args, out_specs=None, scratch=(), aliases=None):
    return pl.pallas_call(
        body,
        out_shape=out_shapes,
        in_specs=specs,
        out_specs=out_specs if out_specs is not None else [VM] * len(out_shapes),
        scratch_shapes=list(scratch),
        input_output_aliases=aliases or {},
        compiler_params=pltpu.CompilerParams(vmem_limit_bytes=VMEM_LIMIT),
    )(*args)


def shape(*dims):
    return jax.ShapeDtypeStruct(dims, F32)


def message_shapes(geo, first):
    extra = 3 if first else 0
    y = shape(2 * geo.nx + extra * geo.nx // 2, SUB, LANES)
    x = shape(2 * HALO + extra * RADIUS, geo.ny, LANES)
    d = shape(2 * RADIUS // 2, SUB, LANES)
    return [y, x, x, d, d]


def pack(geo, fields, extras, messages):
    p, _, sides = geo.place()
    my, me, mo, de, do = messages
    nx = geo.nx

    def ybody(x, carry):
        for f, u in enumerate(fields):
            for i in range(2):
                my[f * nx + x, 4 * i : 4 * i + 4, :] = u[x + HALO, pl.ds(4 + i - 2 * p, 4, stride=SUB), :]
        return carry

    lax.fori_loop(0, nx, ybody, 0, unroll=4)
    if extras:

        def yextra(h, carry):
            for f, u in enumerate(extras):
                for i in range(2):
                    rows = u[2 * h + i + HALO, pl.ds(5 - 3 * p, 4, stride=SUB), :]
                    my[2 * nx + f * (nx // 2) + h, 4 * i : 4 * i + 4, :] = rows
            return carry

        lax.fori_loop(0, nx // 2, yextra, 0, unroll=2)
    for (right, _), mx, md in zip(sides, (me, mo), (de, do)):
        wide = jnp.where(right, nx, HALO)
        thin = jnp.where(right, nx + HALO - RADIUS, HALO)

        def xbody(i, carry, mx=mx, wide=wide):
            for f, u in enumerate(fields):
                for q in range(geo.srows):
                    mx[f * HALO + i, 4 * q : 4 * q + 4, :] = u[wide + i, pl.ds(2 * p + q, 4, stride=SUB), :]
            return carry

        lax.fori_loop(0, HALO, xbody, 0, unroll=2)
        for i in range(RADIUS):
            for f, u in enumerate(extras):
                for q in range(geo.srows):
                    mx[2 * HALO + f * RADIUS + i, 4 * q : 4 * q + 4, :] = u[thin + i, pl.ds(2 * p + q, 4, stride=SUB), :]
            for f, u in enumerate(fields):
                rows = u[thin + i, pl.ds(5 - 3 * p, 4, stride=SUB), :]
                md[2 * f + i // 2, 4 * (i % 2) : 4 * (i % 2) + 4, :] = rows


def unpack(geo, fields, extras, messages):
    p, _, sides = geo.place()
    my, me, mo, de, do = messages
    nx = geo.nx

    def ybody(x, carry):
        for f, u in enumerate(fields):
            for i in range(2):
                u[x + HALO, pl.ds(6 + i - 6 * p, 4, stride=SUB), :] = my[f * nx + x, 4 * i : 4 * i + 4, :]
        return carry

    lax.fori_loop(0, nx, ybody, 0, unroll=4)
    if extras:

        def yextra(h, carry):
            for f, u in enumerate(extras):
                for i in range(2):
                    rows = my[2 * nx + f * (nx // 2) + h, 4 * i : 4 * i + 4, :]
                    u[2 * h + i + HALO, pl.ds(6 - 5 * p, 4, stride=SUB), :] = rows
            return carry

        lax.fori_loop(0, nx // 2, yextra, 0, unroll=2)
    for (right, ok), mx, md in zip(sides, (me, mo), (de, do)):

        @pl.when(ok)
        def _(right=right, mx=mx, md=md):
            wide = jnp.where(right, nx + HALO, 0)
            thin = jnp.where(right, nx + HALO, HALO - RADIUS)

            def xbody(i, carry):
                for f, u in enumerate(fields):
                    for q in range(geo.srows):
                        u[wide + i, pl.ds(2 * p + q, 4, stride=SUB), :] = mx[f * HALO + i, 4 * q : 4 * q + 4, :]
                return carry

            lax.fori_loop(0, HALO, xbody, 0, unroll=2)
            for i in range(RADIUS):
                for f, u in enumerate(extras):
                    for q in range(geo.srows):
                        rows = mx[2 * HALO + f * RADIUS + i, 4 * q : 4 * q + 4, :]
                        u[thin + i, pl.ds(2 * p + q, 4, stride=SUB), :] = rows
                for f, u in enumerate(fields):
                    rows = md[2 * f + i // 2, 4 * (i % 2) : 4 * (i % 2) + 4, :]
                    u[thin + i, pl.ds(6 - 5 * p, 4, stride=SUB), :] = rows


def load_kernel(geo):
    nx, ny, xe = geo.nx, geo.ny, geo.xe

    def body(s0, s1, r0, r1, c0, us, ur, ps, pr, cc, dw, my, me, mo, de, do, pad, sem):
        p, _, _ = geo.place()
        inside = pl.ds(pl.multiple_of(SUB * p, SUB), ny)
        sources = (s0.at[0], r0.at[0], s1.at[0], r1.at[0], c0)
        copies = [
            pltpu.make_async_copy(src, pad.at[f, :, inside, :], sem.at[f]) for f, src in enumerate(sources)
        ]
        for copy in copies:
            copy.start()
        outside = pl.ds(pl.multiple_of(ny - ny * p, SUB), SUB)
        targets = (us, ur, ps, pr, cc)
        row = lax.broadcasted_iota(jnp.int32, (LANES, LANES), 0)
        col = lax.broadcasted_iota(jnp.int32, (LANES, LANES), 1)
        gap = jnp.abs(row - col)
        d = jnp.zeros((LANES, LANES), F32)
        for k in range(1, RADIUS + 1):
            d = jnp.where(gap == k, RATIOS[k], d)
        dw[0:LANES, :] = d.astype(jnp.bfloat16)
        dw[LANES : 2 * LANES, :] = d.astype(jnp.bfloat16)
        zero = jnp.zeros((geo.win, LANES), F32)
        for f, u in enumerate(targets):
            for x in range(nx):
                pad[f, x, outside, :] = jnp.zeros((SUB, LANES), F32)
            for x in range(HALO):
                u[x] = zero
                u[nx + HALO + x] = zero
        for f, (u, copy) in enumerate(zip(targets, copies)):
            copy.wait()

            def turn(x, carry, f=f, u=u):
                for j in range(geo.jn):
                    u[x + HALO, SUB * j : SUB * j + SUB, :] = pad[f, x, pl.ds(j, SUB, stride=geo.jn), :]
                return carry

            lax.fori_loop(0, nx, turn, 0, unroll=4)
        pack(geo, (us, ur), (ps, pr, cc), (my, me, mo, de, do))

    return body


def receiver_kernel(geo, nrec):
    rows_all = geo.xe * geo.win
    block = 128

    def body(ri, rc, traces, wavelet, out, wav, table):
        p, g, _ = geo.place()
        x = ri[...] - g * geo.nx + HALO
        w = rc[...] - p * geo.ny + SUB * p
        ok = (x >= 0) & (x < geo.xe) & (w >= 0) & (w < geo.win)
        shift = geo.jn.bit_length() - 1
        row = x * geo.win + (w & (geo.jn - 1)) * SUB + (w >> shift)
        row = jnp.where(ok, row, -1)
        table[...] = jnp.zeros_like(table)
        table[0:STEPS, :] = traces[0] * (1.0 / COEFFS[1])
        wav[...] = jnp.zeros_like(wav)
        wav[0:1, 0:STEPS] = wavelet[...] * (1.0 / COEFFS[1])
        tab = table[...]

        def chunk(i, carry):
            at = i * block + lax.broadcasted_iota(jnp.int32, (block, nrec), 0)
            hot = jnp.where(at == row, 1.0, 0.0).astype(F32)
            plane = lax.dot_general(
                hot, tab, (((1,), (1,)), ((), ())), precision=lax.Precision.HIGHEST, preferred_element_type=F32
            )
            planes = block // geo.win
            out[pl.ds(i * planes, planes)] = plane.reshape(planes, geo.win, LANES)
            return carry

        lax.fori_loop(0, rows_all // block, chunk, 0)

    return body


def update_planes(geo, pairs, cc, ee, dw, x, moment, gg, corr, fresh):
    jn, span = geo.jn, GROUP * geo.win
    sub = lax.broadcasted_iota(jnp.int32, (SUB, LANES), 0)
    at_depth = lax.broadcasted_iota(jnp.int32, (SUB, LANES), 1) == REC_DEPTH
    first, last = sub == 0, sub == SUB - 1
    rows = jnp.concatenate([u[pl.ds(x, GROUP)].reshape(span, LANES) for u, _ in pairs], axis=0)
    hi = rows.astype(jnp.bfloat16)
    lo = (rows - hi.astype(F32)).astype(jnp.bfloat16)
    deep = jnp.dot(jnp.concatenate([hi, lo], axis=1), dw[...], preferred_element_type=F32)
    for i in range(GROUP):
        news = []
        for f, (u, prior) in enumerate(pairs):
            mid = [u[x + i, SUB * j : SUB * j + SUB, :] for j in range(jn)]
            below = [jnp.where(first, 0.0, pltpu.roll(v, 1, 0)) for v in mid]
            above = [jnp.where(last, 0.0, pltpu.roll(v, SUB - 1, 0)) for v in mid]
            line = below + mid + above
            for j in range(jn):
                tile = slice(SUB * j, SUB * j + SUB)
                at = f * span + i * geo.win + SUB * j
                acc = deep[at : at + SUB]
                if f == 1:
                    fed = pltpu.roll(gg[x + i, tile, :], (REC_DEPTH - moment) % LANES, 1)
                    acc = acc + jnp.where(at_depth, fed, 0.0)
                for k in range(1, RADIUS + 1):
                    near = (u[x + i + k, tile, :] + u[x + i - k, tile, :]) + (line[jn + j + k] + line[jn + j - k])
                    acc = acc + (near if k == 1 else RATIOS[k] * near)
                new = (ee[x + i, tile, :] * mid[j] - prior[x + i, tile, :]) + cc[x + i, tile, :] * acc
                prior[x + i, tile, :] = new
                news.append(new)
        for j in range(jn):
            tile = slice(SUB * j, SUB * j + SUB)
            product = news[j] * news[jn + j]
            if not fresh:
                product = product + corr[x + i - HALO + RADIUS, tile, :]
            corr[x + i - HALO + RADIUS, tile, :] = product


def one_step(geo, moment, us, ur, ps, pr, cc, ee, gg, corr, dw, wav, src, first, count, fresh):
    def group(i, carry):
        x = first + i * GROUP
        update_planes(geo, ((us, ps), (ur, pr)), cc, ee, dw, x, moment, gg, corr, fresh)
        return carry

    lax.fori_loop(0, count // GROUP, group, 0)
    xs, row, ok = src

    @pl.when(ok & (xs >= first) & (xs < first + count))
    def _():
        lane = lax.broadcasted_iota(jnp.int32, (SUB, LANES), 1)
        shot = jnp.where(lane == SRC_DEPTH, pltpu.roll(wav[...], (SRC_DEPTH - moment) % LANES, 1), 0.0)
        add = cc[xs, pl.ds(row, 1), :] * shot[0:1]
        ps[xs, pl.ds(row, 1), :] = ps[xs, pl.ds(row, 1), :] + add
        at = xs - HALO + RADIUS
        corr[at, pl.ds(row, 1), :] = corr[at, pl.ds(row, 1), :] + add * pr[xs, pl.ds(row, 1), :]


def round_kernel(geo, block, last):
    first_round = block == 0

    def body(*refs):
        refs = list(refs)
        take = lambda n: [refs.pop(0) for _ in range(n)]
        take(4)
        if first_round:
            take(1)
        else:
            take(1)
            cc, ee = take(2)
        dw, gg, wav = take(3)
        inputs = take(5)
        sx, sy = take(2)
        us, ur, ps, pr = take(4)
        if first_round:
            cc, ee = take(2)
        (corr,) = take(1)
        outs = [] if last else take(5)
        p, g, _ = geo.place()
        xs = sx[0] - g * geo.nx + HALO
        w = sy[0] - p * geo.ny + SUB * p
        ok = (w >= 0) & (w < geo.win) & (xs >= 0) & (xs < geo.xe)
        shift = geo.jn.bit_length() - 1
        src = (xs, (w & (geo.jn - 1)) * SUB + (w >> shift), ok)
        unpack(geo, (us, ur), (ps, pr, cc) if first_round else (), inputs)
        if first_round:

            def scale(x, carry):
                speed = cc[x]
                ee[x] = 2.0 + (3.0 * COEFFS[0]) * speed
                cc[x] = COEFFS[1] * speed
                return carry

            lax.fori_loop(0, geo.xe, scale, 0, unroll=2)
        common = (cc, ee, gg, corr, dw, wav, src)
        one_step(geo, DEEP * block, us, ur, ps, pr, *common, HALO - RADIUS, geo.nx + 2 * RADIUS, first_round)
        one_step(geo, DEEP * block + 1, ps, pr, us, ur, *common, HALO, geo.nx, False)
        if not last:
            pack(geo, (us, ur), (), outs)

    return body


def corr_kernel(geo, halves):
    part = geo.nx // halves

    def body(corr, mine, other, pad):
        p, _, _ = geo.place()
        q = lax.axis_index("sa")

        def turn(x, carry):
            for j in range(geo.jn):
                pad[x, pl.ds(j, SUB, stride=geo.jn), :] = corr[x + RADIUS, SUB * j : SUB * j + SUB, :]
            return carry

        lax.fori_loop(0, geo.nx, turn, 0, unroll=4)
        inside = pl.ds(pl.multiple_of(SUB * p, SUB), geo.ny)

        def split(x, carry):
            mine[x] = pad[q * part + x, inside, :]
            other[x] = pad[(halves - 1 - q) * part + x, inside, :]
            return carry

        lax.fori_loop(0, part, split, 0, unroll=2)

    return body


def store_kernel(geo):
    def body(us, ur, ps, pr, o0, o1, o2, o3, pad, sem):
        p, _, _ = geo.place()
        inside = pl.ds(pl.multiple_of(SUB * p, SUB), geo.ny)
        copies = []
        for f, (u, o) in enumerate(((us, o0), (ps, o1), (ur, o2), (pr, o3))):

            def turn(x, carry, f=f, u=u):
                for j in range(geo.jn):
                    pad[f, x, pl.ds(j, SUB, stride=geo.jn), :] = u[x + HALO, SUB * j : SUB * j + SUB, :]
                return carry

            lax.fori_loop(0, geo.nx, turn, 0, unroll=4)
            copy = pltpu.make_async_copy(pad.at[f, :, inside, :], o.at[0], sem.at[f])
            copy.start()
            copies.append(copy)
        for copy in copies:
            copy.wait()

    return body


def fast_body(mesh):
    def run(sn, sl, rn, rl, courant, wavelet, traces, si, sc, ri, rc):
        nx, ny, nz = courant.shape
        geo = Geometry(mesh, nx, ny)
        state = shape(geo.xe, geo.win, nz)
        names = mesh.axis_names
        routes = [
            neighbour(mesh, 0, True, False),
            neighbour(mesh, 0, False, True),
            neighbour(mesh, 1, False, True),
            neighbour(mesh, 0, True, True),
            neighbour(mesh, 1, True, True),
        ]
        send = lambda ms: [lax.ppermute(m, names, route) for m, route in zip(ms, routes)]
        loaded = call(
            load_kernel(geo),
            [state] * 5
            + [jax.ShapeDtypeStruct((2 * LANES, LANES), jnp.bfloat16)]
            + message_shapes(geo, True),
            [HBM] * 5,
            (sn, sl, rn, rl, courant),
            scratch=[pltpu.VMEM((5, nx, geo.win, nz), F32), pltpu.SemaphoreType.DMA((5,))],
        )
        us, ur, ps, pr, cc, dw = loaded[:6]
        messages = send(loaded[6:])
        nrec = traces.shape[2]
        gg, wav = call(
            receiver_kernel(geo, nrec),
            [state, shape(SUB, LANES)],
            [VM] * 4,
            (ri, rc, traces, wavelet),
            scratch=[pltpu.VMEM((LANES, nrec), F32)],
        )
        corr_shape = shape(nx + 2 * RADIUS, geo.win, nz)
        corr = ee = None
        blocks = STEPS // DEEP
        for block in range(blocks):
            last = block == blocks - 1
            if block == 0:
                args = [us, ur, ps, pr, cc]
                outs = [state] * 6 + [corr_shape]
                aliases = {i: i for i in range(5)}
            else:
                args = [us, ur, ps, pr, corr, cc, ee]
                outs = [state] * 4 + [corr_shape]
                aliases = {i: i for i in range(5)}
            args = args + [dw, gg, wav] + messages
            outs = call(
                round_kernel(geo, block, last),
                outs + ([] if last else message_shapes(geo, False)),
                [VM] * len(args) + [SM] * 2,
                args + [si, sc],
                aliases=aliases,
            )
            us, ur, ps, pr = outs[:4]
            if block == 0:
                cc, ee, corr = outs[4:7]
            else:
                corr = outs[4]
            if not last:
                messages = send(outs[-5:])
        halves = mesh.shape["sa"]
        part = shape(nx // halves, ny, nz)
        mine, other = call(
            corr_kernel(geo, halves), [part] * 2, [VM], (corr,), scratch=[pltpu.VMEM((nx, geo.win, nz), F32)]
        )
        pairs = [(i, halves - 1 - i) for i in range(halves)]
        image = (mine + lax.ppermute(other, "sa", pairs)) / STEPS
        fields = call(
            store_kernel(geo),
            [shape(1, nx, ny, nz)] * 4,
            [VM] * 4,
            (us, ur, ps, pr),
            out_specs=[HBM] * 4,
            scratch=[pltpu.VMEM((4, nx, geo.win, nz), F32), pltpu.SemaphoreType.DMA((4,))],
        )
        return (*fields, image)

    return run


def padded_2(cells, sides, width):
    for axis, dim in sides:
        count = lax.axis_size(axis)
        ends = count - 1
        head = lax.slice_in_dim(cells, 0, width, axis=dim)
        tail = lax.slice_in_dim(cells, cells.shape[dim] - width, cells.shape[dim], axis=dim)
        cells = jnp.concatenate(
            [
                lax.ppermute(tail, axis, [(i, (i + 1) % count) for i in range(ends)]),
                cells,
                lax.ppermute(head, axis, [((i + 1) % count, i) for i in range(ends)]),
            ],
            axis=dim,
        )
    return cells


def laplace(padded):
    inline_span = padded.shape[0] - 8
    cross_span = padded.shape[1] - 8
    center = padded[4 : 4 + inline_span, 4 : 4 + cross_span]
    depth_span = center.shape[2]
    depth_padded = jnp.pad(center, ((0, 0), (0, 0), (4, 4)))
    summed = 3.0 * COEFFS[0] * center
    for distance in range(1, 5):
        neighbours = (
            padded[4 + distance : 4 + distance + inline_span, 4 : 4 + cross_span]
            + padded[4 - distance : 4 - distance + inline_span, 4 : 4 + cross_span]
        )
        neighbours = (
            neighbours
            + padded[4 : 4 + inline_span, 4 + distance : 4 + distance + cross_span]
            + padded[4 : 4 + inline_span, 4 - distance : 4 - distance + cross_span]
        )
        neighbours = (
            neighbours
            + depth_padded[:, :, 4 + distance : 4 + distance + depth_span]
            + depth_padded[:, :, 4 - distance : 4 - distance + depth_span]
        )
        summed = summed + COEFFS[distance] * neighbours
    return summed


def crop_margin(values, margin_cut):
    if margin_cut == 0:
        return values
    return values[
        margin_cut : values.shape[0] - margin_cut, margin_cut : values.shape[1] - margin_cut
    ]


def general_body(
    source_now,
    source_later,
    receiver_now,
    receiver_later,
    courant,
    wavelet,
    traces,
    source_inline,
    source_crossline,
    receiver_inline,
    receiver_crossline,
):
    inline_count, cross_count, depth_count = courant.shape
    inline_anchor = lax.axis_index("gx") * inline_count
    cross_anchor = lax.axis_index("gy") * cross_count
    inline_extent = inline_count * lax.axis_size("gx")
    cross_extent = cross_count * lax.axis_size("gy")
    depth_axis = jnp.arange(depth_count)
    source_layer = (depth_axis == SRC_DEPTH).astype(jnp.float32)
    receiver_layer = (depth_axis == REC_DEPTH).astype(jnp.float32)
    wavelet_row = wavelet[0]
    records = traces[0]
    source_field = source_now[0]
    source_prior = source_later[0]
    receiver_field = receiver_now[0]
    receiver_prior = receiver_later[0]
    correlation = jnp.zeros(courant.shape, jnp.float32)
    widest = 4 * (GENERAL_BLOCK - 1)
    speed_wide = padded_2(courant, (("gx", 0), ("gy", 1)), widest)
    inline_cells = inline_anchor - widest + jnp.arange(inline_count + 2 * widest)
    cross_cells = cross_anchor - widest + jnp.arange(cross_count + 2 * widest)
    inline_hot = (inline_cells[:, None] == receiver_inline[0][None, :]).astype(jnp.float32)
    cross_hot = (receiver_crossline[0][:, None] == cross_cells[None, :]).astype(jnp.float32)
    receivers = cross_hot.shape[0]
    weighted = (records.T[:, :, None] * cross_hot[:, None, :]).reshape(
        receivers, STEPS * cross_hot.shape[1]
    )
    planes = jnp.dot(inline_hot, weighted, precision=lax.Precision.HIGHEST).reshape(
        inline_hot.shape[0], STEPS, cross_hot.shape[1]
    )
    source_spot = (inline_cells == source_inline[0]).astype(jnp.float32)[:, None] * (
        cross_cells == source_crossline[0]
    ).astype(jnp.float32)[None, :]
    inline_in = ((inline_cells >= 0) & (inline_cells < inline_extent)).astype(jnp.float32)
    cross_in = ((cross_cells >= 0) & (cross_cells < cross_extent)).astype(jnp.float32)
    inside = inline_in[:, None, None] * cross_in[None, :, None]
    planes, source_spot, inside = (planes, source_spot, inside)
    for segment in range(GENERAL_BLOCKS):
        source_wide, receiver_wide = (
            padded_2(source_field, (("gx", 0), ("gy", 1)), 4 * GENERAL_BLOCK),
            padded_2(receiver_field, (("gx", 0), ("gy", 1)), 4 * GENERAL_BLOCK),
        )
        source_back, receiver_back = (
            padded_2(source_prior, (("gx", 0), ("gy", 1)), widest),
            padded_2(receiver_prior, (("gx", 0), ("gy", 1)), widest),
        )
        for substep in range(GENERAL_BLOCK):
            margin = 4 * (GENERAL_BLOCK - 1 - substep)
            offset = widest - margin
            moment = segment * GENERAL_BLOCK + substep
            speed = crop_margin(speed_wide, offset)
            region = crop_margin(inside, offset)
            record_plane = crop_margin(planes[:, moment, :], offset)
            spot_plane = crop_margin(source_spot, offset)
            source_centre = crop_margin(source_wide, 4)
            receiver_centre = crop_margin(receiver_wide, 4)
            source_new = region * (
                2.0 * source_centre
                - source_back
                + speed
                * (
                    laplace(source_wide)
                    + (wavelet_row[moment] * spot_plane)[:, :, None] * source_layer
                )
            )
            receiver_new = region * (
                2.0 * receiver_centre
                - receiver_back
                + speed * (laplace(receiver_wide) + record_plane[:, :, None] * receiver_layer)
            )
            correlation = correlation + crop_margin(source_new, margin) * crop_margin(
                receiver_new, margin
            )
            source_wide, receiver_wide = (source_new, receiver_new)
            if margin > 0:
                source_back = crop_margin(source_centre, 4)
                receiver_back = crop_margin(receiver_centre, 4)
            else:
                source_back = source_centre
                receiver_back = receiver_centre
        source_field, source_prior = (source_wide, source_back)
        receiver_field, receiver_prior = (receiver_wide, receiver_back)
    image_part = lax.psum_scatter(correlation, "sa", scatter_dimension=0, tiled=True) / STEPS
    return (
        source_field[None],
        source_prior[None],
        receiver_field[None],
        receiver_prior[None],
        image_part,
    )


def any_body(mesh):
    fast = fast_body(mesh)

    def run(*args):
        nx, ny, nz = args[4].shape
        fits = mesh.shape["gy"] == 2 and mesh.shape["sa"] == 2 and nz == LANES
        fits = fits and (ny + HALO) == RADIUS * SUB and nx % (2 * HALO) == 0
        return (fast if fits else general_body)(*args)

    return run


def solution(mesh):
    in_specs = (
        P(("groups", "sa"), "gx", "gy", None),
        P(("groups", "sa"), "gx", "gy", None),
        P(("groups", "sa"), "gx", "gy", None),
        P(("groups", "sa"), "gx", "gy", None),
        P("gx", "gy", None),
        P(("groups", "sa"), None),
        P(("groups", "sa"), None, None),
        P(("groups", "sa")),
        P(("groups", "sa")),
        P(("groups", "sa"), None),
        P(("groups", "sa"), None),
    )
    out_specs = (
        P(("groups", "sa"), "gx", "gy", None),
        P(("groups", "sa"), "gx", "gy", None),
        P(("groups", "sa"), "gx", "gy", None),
        P(("groups", "sa"), "gx", "gy", None),
        P(("groups", "gx", "sa"), "gy", None),
    )
    return jax.shard_map(any_body(mesh), mesh=mesh, in_specs=in_specs, out_specs=out_specs, check_vma=False)
```

```python
import itertools

import jax
import jax.numpy as jnp
from jax import lax
from jax.experimental import pallas as pl
from jax.experimental.pallas import tpu as pltpu
from jax.sharding import PartitionSpec as P

SRC_DEPTH = 3
REC_DEPTH = 2
STEPS = 12
COEFFS = (-205.0 / 72.0, 8.0 / 5.0, -1.0 / 5.0, 8.0 / 315.0, -1.0 / 560.0)
RADIUS = 4
LANES = 128
SUB = 8
DEEP = 2
HALO = RADIUS * DEEP
GROUP = 8
RATIOS = [c / COEFFS[1] for c in COEFFS]
GENERAL_BLOCK = 4
GENERAL_BLOCKS = 3
VMEM_LIMIT = 24 << 20

VM = pl.BlockSpec(memory_space=pltpu.VMEM)
SM = pl.BlockSpec(memory_space=pltpu.SMEM)
HBM = pl.BlockSpec(memory_space=pltpu.HBM)
F32 = jnp.float32


class Geometry:
    def __init__(self, mesh, nx, ny):
        self.mesh = mesh
        self.nx, self.ny = nx, ny
        self.xe = nx + 2 * HALO
        self.win = ny + HALO
        self.jn = self.win // SUB
        self.gx = mesh.shape["gx"]
        self.srows = ny // self.jn

    def place(self):
        p = lax.axis_index("gy")
        g = lax.axis_index("gx")
        odd = g % 2
        even_right = odd == 0
        even_ok = jnp.logical_or(odd == 1, g + 1 < self.gx)
        odd_right = odd == 1
        odd_ok = jnp.logical_or(jnp.logical_and(odd == 1, g + 1 < self.gx), jnp.logical_and(odd == 0, g > 0))
        return p, g, ((even_right, even_ok), (odd_right, odd_ok))


def permutation(mesh, move):
    names = mesh.axis_names
    sizes = [mesh.shape[n] for n in names]
    pairs = []
    for idx in itertools.product(*[range(s) for s in sizes]):
        at = dict(zip(names, idx))
        to = move(dict(at))
        if to is None:
            to = dict(at)
            to["sa"] = (mesh.shape["sa"] - 1) - at["sa"]
        a = b = 0
        for n, s in zip(names, sizes):
            a, b = a * s + at[n], b * s + to[n]
        pairs.append((a, b))
    return pairs


def neighbour(mesh, parity, flip_y, step_x):
    count = mesh.shape["gx"]

    def move(at):
        if step_x:
            to = at["gx"] + 1 if at["gx"] % 2 == parity else at["gx"] - 1
            if to < 0 or to >= count:
                return None
            at["gx"] = to
        if flip_y:
            at["gy"] = 1 - at["gy"]
        return at

    return permutation(mesh, move)


def call(body, out_shapes, specs, args, out_specs=None, scratch=(), aliases=None):
    return pl.pallas_call(
        body,
        out_shape=out_shapes,
        in_specs=specs,
        out_specs=out_specs if out_specs is not None else [VM] * len(out_shapes),
        scratch_shapes=list(scratch),
        input_output_aliases=aliases or {},
        compiler_params=pltpu.CompilerParams(vmem_limit_bytes=VMEM_LIMIT),
    )(*args)


def shape(*dims):
    return jax.ShapeDtypeStruct(dims, F32)


def message_shapes(geo, first):
    extra = 3 if first else 0
    y = shape(2 * geo.nx + extra * geo.nx // 2, SUB, LANES)
    x = shape(2 * HALO + extra * RADIUS, geo.ny, LANES)
    d = shape(2 * RADIUS // 2, SUB, LANES)
    return [y, x, x, d, d]


def pack(geo, fields, extras, messages):
    p, _, sides = geo.place()
    my, me, mo, de, do = messages
    nx = geo.nx

    def ybody(x, carry):
        for f, u in enumerate(fields):
            for i in range(2):
                my[f * nx + x, 4 * i : 4 * i + 4, :] = u[x + HALO, pl.ds(4 + i - 2 * p, 4, stride=SUB), :]
        return carry

    lax.fori_loop(0, nx, ybody, 0, unroll=16)
    if extras:

        def yextra(h, carry):
            for f, u in enumerate(extras):
                for i in range(2):
                    rows = u[2 * h + i + HALO, pl.ds(5 - 3 * p, 4, stride=SUB), :]
                    my[2 * nx + f * (nx // 2) + h, 4 * i : 4 * i + 4, :] = rows
            return carry

        lax.fori_loop(0, nx // 2, yextra, 0, unroll=2)
    for (right, _), mx, md in zip(sides, (me, mo), (de, do)):
        wide = jnp.where(right, nx, HALO)
        thin = jnp.where(right, nx + HALO - RADIUS, HALO)

        def xbody(i, carry, mx=mx, wide=wide):
            for f, u in enumerate(fields):
                for q in range(geo.srows):
                    mx[f * HALO + i, 4 * q : 4 * q + 4, :] = u[wide + i, pl.ds(2 * p + q, 4, stride=SUB), :]
            return carry

        lax.fori_loop(0, HALO, xbody, 0, unroll=8)
        for i in range(RADIUS):
            for f, u in enumerate(extras):
                for q in range(geo.srows):
                    mx[2 * HALO + f * RADIUS + i, 4 * q : 4 * q + 4, :] = u[thin + i, pl.ds(2 * p + q, 4, stride=SUB), :]
            for f, u in enumerate(fields):
                rows = u[thin + i, pl.ds(5 - 3 * p, 4, stride=SUB), :]
                md[2 * f + i // 2, 4 * (i % 2) : 4 * (i % 2) + 4, :] = rows


def unpack(geo, fields, extras, messages):
    p, _, sides = geo.place()
    my, me, mo, de, do = messages
    nx = geo.nx

    def ybody(x, carry):
        for f, u in enumerate(fields):
            for i in range(2):
                u[x + HALO, pl.ds(6 + i - 6 * p, 4, stride=SUB), :] = my[f * nx + x, 4 * i : 4 * i + 4, :]
        return carry

    lax.fori_loop(0, nx, ybody, 0, unroll=16)
    if extras:

        def yextra(h, carry):
            for f, u in enumerate(extras):
                for i in range(2):
                    rows = my[2 * nx + f * (nx // 2) + h, 4 * i : 4 * i + 4, :]
                    u[2 * h + i + HALO, pl.ds(6 - 5 * p, 4, stride=SUB), :] = rows
            return carry

        lax.fori_loop(0, nx // 2, yextra, 0, unroll=2)
    for (right, ok), mx, md in zip(sides, (me, mo), (de, do)):

        @pl.when(ok)
        def _(right=right, mx=mx, md=md):
            wide = jnp.where(right, nx + HALO, 0)
            thin = jnp.where(right, nx + HALO, HALO - RADIUS)

            def xbody(i, carry):
                for f, u in enumerate(fields):
                    for q in range(geo.srows):
                        u[wide + i, pl.ds(2 * p + q, 4, stride=SUB), :] = mx[f * HALO + i, 4 * q : 4 * q + 4, :]
                return carry

            lax.fori_loop(0, HALO, xbody, 0, unroll=8)
            for i in range(RADIUS):
                for f, u in enumerate(extras):
                    for q in range(geo.srows):
                        rows = mx[2 * HALO + f * RADIUS + i, 4 * q : 4 * q + 4, :]
                        u[thin + i, pl.ds(2 * p + q, 4, stride=SUB), :] = rows
                for f, u in enumerate(fields):
                    rows = md[2 * f + i // 2, 4 * (i % 2) : 4 * (i % 2) + 4, :]
                    u[thin + i, pl.ds(6 - 5 * p, 4, stride=SUB), :] = rows


def load_kernel(geo):
    nx, ny, xe = geo.nx, geo.ny, geo.xe

    def body(s0, s1, r0, r1, c0, us, ur, ps, pr, cc, dw, my, me, mo, de, do, pad, sem):
        p, _, _ = geo.place()
        inside = pl.ds(pl.multiple_of(SUB * p, SUB), ny)
        sources = (s0.at[0], r0.at[0], s1.at[0], r1.at[0], c0)
        copies = [
            pltpu.make_async_copy(src, pad.at[f, :, inside, :], sem.at[f]) for f, src in enumerate(sources)
        ]
        for copy in copies:
            copy.start()
        outside = pl.ds(pl.multiple_of(ny - ny * p, SUB), SUB)
        targets = (us, ur, ps, pr, cc)
        row = lax.broadcasted_iota(jnp.int32, (LANES, LANES), 0)
        col = lax.broadcasted_iota(jnp.int32, (LANES, LANES), 1)
        gap = jnp.abs(row - col)
        d = jnp.zeros((LANES, LANES), F32)
        for k in range(1, RADIUS + 1):
            d = jnp.where(gap == k, RATIOS[k], d)
        dw[0:LANES, :] = d.astype(jnp.bfloat16)
        dw[LANES : 2 * LANES, :] = d.astype(jnp.bfloat16)
        zero = jnp.zeros((geo.win, LANES), F32)
        for f, u in enumerate(targets):
            for x in range(nx):
                pad[f, x, outside, :] = jnp.zeros((SUB, LANES), F32)
            for x in range(HALO):
                u[x] = zero
                u[nx + HALO + x] = zero
        for f, (u, copy) in enumerate(zip(targets, copies)):
            copy.wait()

            def turn(x, carry, f=f, u=u):
                for j in range(geo.jn):
                    u[x + HALO, SUB * j : SUB * j + SUB, :] = pad[f, x, pl.ds(j, SUB, stride=geo.jn), :]
                return carry

            lax.fori_loop(0, nx, turn, 0, unroll=4)
        pack(geo, (us, ur), (ps, pr, cc), (my, me, mo, de, do))

    return body


def receiver_kernel(geo, nrec):
    rows_all = geo.xe * geo.win
    block = 256

    def body(ri, rc, traces, wavelet, out, wav, table):
        p, g, _ = geo.place()
        x = ri[...] - g * geo.nx + HALO
        w = rc[...] - p * geo.ny + SUB * p
        ok = (x >= 0) & (x < geo.xe) & (w >= 0) & (w < geo.win)
        shift = geo.jn.bit_length() - 1
        row = x * geo.win + (w & (geo.jn - 1)) * SUB + (w >> shift)
        row = jnp.where(ok, row, -1)
        table[...] = jnp.zeros_like(table)
        table[0:STEPS, :] = traces[0] * (1.0 / COEFFS[1])
        wav[...] = jnp.zeros_like(wav)
        wav[0:1, 0:STEPS] = wavelet[...] * (1.0 / COEFFS[1])
        part, left = [], table[...]
        for _ in range(3):
            part.append(left.astype(jnp.bfloat16))
            left = left - part[-1].astype(F32)
        parts = jnp.concatenate(part, axis=1)

        def chunk(i, carry):
            at = i * block + lax.broadcasted_iota(jnp.int32, (block, nrec), 0)
            hot = jnp.where(at == row, 1.0, 0.0).astype(jnp.bfloat16)
            hots = jnp.concatenate([hot, hot, hot], axis=1)
            plane = lax.dot_general(hots, parts, (((1,), (1,)), ((), ())), preferred_element_type=F32)
            planes = block // geo.win
            out[pl.ds(i * planes, planes)] = plane.reshape(planes, geo.win, LANES)
            return carry

        lax.fori_loop(0, rows_all // block, chunk, 0)

    return body


def update_planes(geo, pairs, cc, ee, dw, x, moment, gg, corr, fresh):
    jn, span = geo.jn, GROUP * geo.win
    sub = lax.broadcasted_iota(jnp.int32, (SUB, LANES), 0)
    at_depth = lax.broadcasted_iota(jnp.int32, (SUB, LANES), 1) == REC_DEPTH
    first, last = sub == 0, sub == SUB - 1
    rows = jnp.concatenate([u[pl.ds(x, GROUP)].reshape(span, LANES) for u, _ in pairs], axis=0)
    hi = rows.astype(jnp.bfloat16)
    lo = (rows - hi.astype(F32)).astype(jnp.bfloat16)
    deep = jnp.dot(jnp.concatenate([hi, lo], axis=1), dw[...], preferred_element_type=F32)
    for i in range(GROUP):
        news = []
        for f, (u, prior) in enumerate(pairs):
            mid = [u[x + i, SUB * j : SUB * j + SUB, :] for j in range(jn)]
            below = [jnp.where(first, 0.0, pltpu.roll(v, 1, 0)) for v in mid]
            above = [jnp.where(last, 0.0, pltpu.roll(v, SUB - 1, 0)) for v in mid]
            line = below + mid + above
            for j in range(jn):
                tile = slice(SUB * j, SUB * j + SUB)
                at = f * span + i * geo.win + SUB * j
                acc = deep[at : at + SUB]
                if f == 1:
                    fed = pltpu.roll(gg[x + i, tile, :], (REC_DEPTH - moment) % LANES, 1)
                    acc = acc + jnp.where(at_depth, fed, 0.0)
                for k in range(1, RADIUS + 1):
                    near = (u[x + i + k, tile, :] + u[x + i - k, tile, :]) + (line[jn + j + k] + line[jn + j - k])
                    acc = acc + (near if k == 1 else RATIOS[k] * near)
                new = (ee[x + i, tile, :] * mid[j] - prior[x + i, tile, :]) + cc[x + i, tile, :] * acc
                prior[x + i, tile, :] = new
                news.append(new)
        for j in range(jn):
            tile = slice(SUB * j, SUB * j + SUB)
            product = news[j] * news[jn + j]
            if not fresh:
                product = product + corr[x + i - HALO + RADIUS, tile, :]
            corr[x + i - HALO + RADIUS, tile, :] = product


def one_step(geo, moment, us, ur, ps, pr, cc, ee, gg, corr, dw, wav, src, first, count, fresh):
    def group(i, carry):
        x = first + i * GROUP
        update_planes(geo, ((us, ps), (ur, pr)), cc, ee, dw, x, moment, gg, corr, fresh)
        return carry

    lax.fori_loop(0, count // GROUP, group, 0)
    xs, row, ok = src

    @pl.when(ok & (xs >= first) & (xs < first + count))
    def _():
        lane = lax.broadcasted_iota(jnp.int32, (SUB, LANES), 1)
        shot = jnp.where(lane == SRC_DEPTH, pltpu.roll(wav[...], (SRC_DEPTH - moment) % LANES, 1), 0.0)
        add = cc[xs, pl.ds(row, 1), :] * shot[0:1]
        ps[xs, pl.ds(row, 1), :] = ps[xs, pl.ds(row, 1), :] + add
        at = xs - HALO + RADIUS
        corr[at, pl.ds(row, 1), :] = corr[at, pl.ds(row, 1), :] + add * pr[xs, pl.ds(row, 1), :]


def round_kernel(geo, block, last):
    first_round = block == 0

    def body(*refs):
        refs = list(refs)
        take = lambda n: [refs.pop(0) for _ in range(n)]
        take(4)
        if first_round:
            take(1)
        else:
            take(1)
            cc, ee = take(2)
        dw, gg, wav = take(3)
        inputs = take(5)
        sx, sy = take(2)
        us, ur, ps, pr = take(4)
        if first_round:
            cc, ee = take(2)
        (corr,) = take(1)
        outs = [] if last else take(5)
        p, g, _ = geo.place()
        xs = sx[0] - g * geo.nx + HALO
        w = sy[0] - p * geo.ny + SUB * p
        ok = (w >= 0) & (w < geo.win) & (xs >= 0) & (xs < geo.xe)
        shift = geo.jn.bit_length() - 1
        src = (xs, (w & (geo.jn - 1)) * SUB + (w >> shift), ok)
        unpack(geo, (us, ur), (ps, pr, cc) if first_round else (), inputs)
        if first_round:

            def scale(x, carry):
                speed = cc[x]
                ee[x] = 2.0 + (3.0 * COEFFS[0]) * speed
                cc[x] = COEFFS[1] * speed
                return carry

            lax.fori_loop(0, geo.xe, scale, 0, unroll=2)
        common = (cc, ee, gg, corr, dw, wav, src)
        one_step(geo, DEEP * block, us, ur, ps, pr, *common, HALO - RADIUS, geo.nx + 2 * RADIUS, first_round)
        one_step(geo, DEEP * block + 1, ps, pr, us, ur, *common, HALO, geo.nx, False)
        if not last:
            pack(geo, (us, ur), (), outs)

    return body


def corr_kernel(geo, halves):
    part = geo.nx // halves

    def body(corr, mine, other, pad):
        p, _, _ = geo.place()
        q = lax.axis_index("sa")

        def turn(x, carry):
            for j in range(geo.jn):
                pad[x, pl.ds(j, SUB, stride=geo.jn), :] = corr[x + RADIUS, SUB * j : SUB * j + SUB, :]
            return carry

        lax.fori_loop(0, geo.nx, turn, 0, unroll=4)
        inside = pl.ds(pl.multiple_of(SUB * p, SUB), geo.ny)

        def split(x, carry):
            mine[x] = pad[q * part + x, inside, :]
            other[x] = pad[(halves - 1 - q) * part + x, inside, :]
            return carry

        lax.fori_loop(0, part, split, 0, unroll=2)

    return body


def store_kernel(geo):
    def body(us, ur, ps, pr, o0, o1, o2, o3, pad, sem):
        p, _, _ = geo.place()
        inside = pl.ds(pl.multiple_of(SUB * p, SUB), geo.ny)
        copies = []
        for f, (u, o) in enumerate(((us, o0), (ps, o1), (ur, o2), (pr, o3))):

            def turn(x, carry, f=f, u=u):
                for j in range(geo.jn):
                    pad[f, x, pl.ds(j, SUB, stride=geo.jn), :] = u[x + HALO, SUB * j : SUB * j + SUB, :]
                return carry

            lax.fori_loop(0, geo.nx, turn, 0, unroll=4)
            copy = pltpu.make_async_copy(pad.at[f, :, inside, :], o.at[0], sem.at[f])
            copy.start()
            copies.append(copy)
        for copy in copies:
            copy.wait()

    return body


def fast_body(mesh):
    def run(sn, sl, rn, rl, courant, wavelet, traces, si, sc, ri, rc):
        nx, ny, nz = courant.shape
        geo = Geometry(mesh, nx, ny)
        state = shape(geo.xe, geo.win, nz)
        names = mesh.axis_names
        routes = [
            neighbour(mesh, 0, True, False),
            neighbour(mesh, 0, False, True),
            neighbour(mesh, 1, False, True),
            neighbour(mesh, 0, True, True),
            neighbour(mesh, 1, True, True),
        ]
        send = lambda ms: [lax.ppermute(m, names, route) for m, route in zip(ms, routes)]
        loaded = call(
            load_kernel(geo),
            [state] * 5
            + [jax.ShapeDtypeStruct((2 * LANES, LANES), jnp.bfloat16)]
            + message_shapes(geo, True),
            [HBM] * 5,
            tuple(pltpu.with_memory_space_constraint(v, pltpu.HBM) for v in (sn, sl, rn, rl, courant)),
            scratch=[pltpu.VMEM((5, nx, geo.win, nz), F32), pltpu.SemaphoreType.DMA((5,))],
        )
        us, ur, ps, pr, cc, dw = loaded[:6]
        messages = send(loaded[6:])
        nrec = traces.shape[2]
        gg, wav = call(
            receiver_kernel(geo, nrec),
            [state, shape(SUB, LANES)],
            [VM] * 4,
            (ri, rc, traces, wavelet),
            scratch=[pltpu.VMEM((LANES, nrec), F32)],
        )
        corr_shape = shape(nx + 2 * RADIUS, geo.win, nz)
        corr = ee = None
        blocks = STEPS // DEEP
        for block in range(blocks):
            last = block == blocks - 1
            if block == 0:
                args = [us, ur, ps, pr, cc]
                outs = [state] * 6 + [corr_shape]
                aliases = {i: i for i in range(5)}
            else:
                args = [us, ur, ps, pr, corr, cc, ee]
                outs = [state] * 4 + [corr_shape]
                aliases = {i: i for i in range(5)}
            args = args + [dw, gg, wav] + messages
            outs = call(
                round_kernel(geo, block, last),
                outs + ([] if last else message_shapes(geo, False)),
                [VM] * len(args) + [SM] * 2,
                args + [si, sc],
                aliases=aliases,
            )
            us, ur, ps, pr = outs[:4]
            if block == 0:
                cc, ee, corr = outs[4:7]
            else:
                corr = outs[4]
            if not last:
                messages = send(outs[-5:])
        halves = mesh.shape["sa"]
        part = shape(nx // halves, ny, nz)
        mine, other = call(
            corr_kernel(geo, halves), [part] * 2, [VM], (corr,), scratch=[pltpu.VMEM((nx, geo.win, nz), F32)]
        )
        pairs = [(i, halves - 1 - i) for i in range(halves)]
        image = (mine + lax.ppermute(other, "sa", pairs)) / STEPS
        fields = call(
            store_kernel(geo),
            [shape(1, nx, ny, nz)] * 4,
            [VM] * 4,
            (us, ur, ps, pr),
            out_specs=[HBM] * 4,
            scratch=[pltpu.VMEM((4, nx, geo.win, nz), F32), pltpu.SemaphoreType.DMA((4,))],
        )
        return (*fields, image)

    return run


def padded_2(cells, sides, width):
    for axis, dim in sides:
        count = lax.axis_size(axis)
        ends = count - 1
        head = lax.slice_in_dim(cells, 0, width, axis=dim)
        tail = lax.slice_in_dim(cells, cells.shape[dim] - width, cells.shape[dim], axis=dim)
        cells = jnp.concatenate(
            [
                lax.ppermute(tail, axis, [(i, (i + 1) % count) for i in range(ends)]),
                cells,
                lax.ppermute(head, axis, [((i + 1) % count, i) for i in range(ends)]),
            ],
            axis=dim,
        )
    return cells


def laplace(padded):
    inline_span = padded.shape[0] - 8
    cross_span = padded.shape[1] - 8
    center = padded[4 : 4 + inline_span, 4 : 4 + cross_span]
    depth_span = center.shape[2]
    depth_padded = jnp.pad(center, ((0, 0), (0, 0), (4, 4)))
    summed = 3.0 * COEFFS[0] * center
    for distance in range(1, 5):
        neighbours = (
            padded[4 + distance : 4 + distance + inline_span, 4 : 4 + cross_span]
            + padded[4 - distance : 4 - distance + inline_span, 4 : 4 + cross_span]
        )
        neighbours = (
            neighbours
            + padded[4 : 4 + inline_span, 4 + distance : 4 + distance + cross_span]
            + padded[4 : 4 + inline_span, 4 - distance : 4 - distance + cross_span]
        )
        neighbours = (
            neighbours
            + depth_padded[:, :, 4 + distance : 4 + distance + depth_span]
            + depth_padded[:, :, 4 - distance : 4 - distance + depth_span]
        )
        summed = summed + COEFFS[distance] * neighbours
    return summed


def crop_margin(values, margin_cut):
    if margin_cut == 0:
        return values
    return values[
        margin_cut : values.shape[0] - margin_cut, margin_cut : values.shape[1] - margin_cut
    ]


def general_body(
    source_now,
    source_later,
    receiver_now,
    receiver_later,
    courant,
    wavelet,
    traces,
    source_inline,
    source_crossline,
    receiver_inline,
    receiver_crossline,
):
    inline_count, cross_count, depth_count = courant.shape
    inline_anchor = lax.axis_index("gx") * inline_count
    cross_anchor = lax.axis_index("gy") * cross_count
    inline_extent = inline_count * lax.axis_size("gx")
    cross_extent = cross_count * lax.axis_size("gy")
    depth_axis = jnp.arange(depth_count)
    source_layer = (depth_axis == SRC_DEPTH).astype(jnp.float32)
    receiver_layer = (depth_axis == REC_DEPTH).astype(jnp.float32)
    wavelet_row = wavelet[0]
    records = traces[0]
    source_field = source_now[0]
    source_prior = source_later[0]
    receiver_field = receiver_now[0]
    receiver_prior = receiver_later[0]
    correlation = jnp.zeros(courant.shape, jnp.float32)
    widest = 4 * (GENERAL_BLOCK - 1)
    speed_wide = padded_2(courant, (("gx", 0), ("gy", 1)), widest)
    inline_cells = inline_anchor - widest + jnp.arange(inline_count + 2 * widest)
    cross_cells = cross_anchor - widest + jnp.arange(cross_count + 2 * widest)
    inline_hot = (inline_cells[:, None] == receiver_inline[0][None, :]).astype(jnp.float32)
    cross_hot = (receiver_crossline[0][:, None] == cross_cells[None, :]).astype(jnp.float32)
    receivers = cross_hot.shape[0]
    weighted = (records.T[:, :, None] * cross_hot[:, None, :]).reshape(
        receivers, STEPS * cross_hot.shape[1]
    )
    planes = jnp.dot(inline_hot, weighted, precision=lax.Precision.HIGHEST).reshape(
        inline_hot.shape[0], STEPS, cross_hot.shape[1]
    )
    source_spot = (inline_cells == source_inline[0]).astype(jnp.float32)[:, None] * (
        cross_cells == source_crossline[0]
    ).astype(jnp.float32)[None, :]
    inline_in = ((inline_cells >= 0) & (inline_cells < inline_extent)).astype(jnp.float32)
    cross_in = ((cross_cells >= 0) & (cross_cells < cross_extent)).astype(jnp.float32)
    inside = inline_in[:, None, None] * cross_in[None, :, None]
    planes, source_spot, inside = (planes, source_spot, inside)
    for segment in range(GENERAL_BLOCKS):
        source_wide, receiver_wide = (
            padded_2(source_field, (("gx", 0), ("gy", 1)), 4 * GENERAL_BLOCK),
            padded_2(receiver_field, (("gx", 0), ("gy", 1)), 4 * GENERAL_BLOCK),
        )
        source_back, receiver_back = (
            padded_2(source_prior, (("gx", 0), ("gy", 1)), widest),
            padded_2(receiver_prior, (("gx", 0), ("gy", 1)), widest),
        )
        for substep in range(GENERAL_BLOCK):
            margin = 4 * (GENERAL_BLOCK - 1 - substep)
            offset = widest - margin
            moment = segment * GENERAL_BLOCK + substep
            speed = crop_margin(speed_wide, offset)
            region = crop_margin(inside, offset)
            record_plane = crop_margin(planes[:, moment, :], offset)
            spot_plane = crop_margin(source_spot, offset)
            source_centre = crop_margin(source_wide, 4)
            receiver_centre = crop_margin(receiver_wide, 4)
            source_new = region * (
                2.0 * source_centre
                - source_back
                + speed
                * (
                    laplace(source_wide)
                    + (wavelet_row[moment] * spot_plane)[:, :, None] * source_layer
                )
            )
            receiver_new = region * (
                2.0 * receiver_centre
                - receiver_back
                + speed * (laplace(receiver_wide) + record_plane[:, :, None] * receiver_layer)
            )
            correlation = correlation + crop_margin(source_new, margin) * crop_margin(
                receiver_new, margin
            )
            source_wide, receiver_wide = (source_new, receiver_new)
            if margin > 0:
                source_back = crop_margin(source_centre, 4)
                receiver_back = crop_margin(receiver_centre, 4)
            else:
                source_back = source_centre
                receiver_back = receiver_centre
        source_field, source_prior = (source_wide, source_back)
        receiver_field, receiver_prior = (receiver_wide, receiver_back)
    image_part = lax.psum_scatter(correlation, "sa", scatter_dimension=0, tiled=True) / STEPS
    return (
        source_field[None],
        source_prior[None],
        receiver_field[None],
        receiver_prior[None],
        image_part,
    )


def any_body(mesh):
    fast = fast_body(mesh)

    def run(*args):
        nx, ny, nz = args[4].shape
        fits = mesh.shape["gy"] == 2 and mesh.shape["sa"] == 2 and nz == LANES
        fits = fits and (ny + HALO) == RADIUS * SUB and nx % (2 * HALO) == 0
        return (fast if fits else general_body)(*args)

    return run


def solution(mesh):
    in_specs = (
        P(("groups", "sa"), "gx", "gy", None),
        P(("groups", "sa"), "gx", "gy", None),
        P(("groups", "sa"), "gx", "gy", None),
        P(("groups", "sa"), "gx", "gy", None),
        P("gx", "gy", None),
        P(("groups", "sa"), None),
        P(("groups", "sa"), None, None),
        P(("groups", "sa")),
        P(("groups", "sa")),
        P(("groups", "sa"), None),
        P(("groups", "sa"), None),
    )
    out_specs = (
        P(("groups", "sa"), "gx", "gy", None),
        P(("groups", "sa"), "gx", "gy", None),
        P(("groups", "sa"), "gx", "gy", None),
        P(("groups", "sa"), "gx", "gy", None),
        P(("groups", "gx", "sa"), "gy", None),
    )
    return jax.shard_map(any_body(mesh), mesh=mesh, in_specs=in_specs, out_specs=out_specs, check_vma=False)
```

```python
import itertools

import jax
import jax.numpy as jnp
from jax import lax
from jax.experimental import pallas as pl
from jax.experimental.pallas import tpu as pltpu
from jax.sharding import PartitionSpec as P

SRC_DEPTH = 3
REC_DEPTH = 2
STEPS = 12
COEFFS = (-205.0 / 72.0, 8.0 / 5.0, -1.0 / 5.0, 8.0 / 315.0, -1.0 / 560.0)
RADIUS = 4
LANES = 128
SUB = 8
DEEP = 2
HALO = RADIUS * DEEP
TRIPS = 1
FAR = (3, 4)
RATIOS = [c / COEFFS[1] for c in COEFFS]
GENERAL_BLOCK = 4
GENERAL_BLOCKS = 3
VMEM_LIMIT = 24 << 20

VM = pl.BlockSpec(memory_space=pltpu.VMEM)
SM = pl.BlockSpec(memory_space=pltpu.SMEM)
HBM = pl.BlockSpec(memory_space=pltpu.HBM)
F32 = jnp.float32


class Geometry:
    def __init__(self, mesh, nx, ny):
        self.mesh = mesh
        self.nx, self.ny = nx, ny
        self.xe = nx + 2 * HALO
        self.win = ny + HALO
        self.jn = self.win // SUB
        self.gx = mesh.shape["gx"]
        self.srows = ny // self.jn

    def place(self):
        p = lax.axis_index("gy")
        g = lax.axis_index("gx")
        odd = g % 2
        even_right = odd == 0
        even_ok = jnp.logical_or(odd == 1, g + 1 < self.gx)
        odd_right = odd == 1
        odd_ok = jnp.logical_or(jnp.logical_and(odd == 1, g + 1 < self.gx), jnp.logical_and(odd == 0, g > 0))
        return p, g, ((even_right, even_ok), (odd_right, odd_ok))


def permutation(mesh, move):
    names = mesh.axis_names
    sizes = [mesh.shape[n] for n in names]
    pairs = []
    for idx in itertools.product(*[range(s) for s in sizes]):
        at = dict(zip(names, idx))
        to = move(dict(at))
        if to is None:
            to = dict(at)
            to["sa"] = (mesh.shape["sa"] - 1) - at["sa"]
        a = b = 0
        for n, s in zip(names, sizes):
            a, b = a * s + at[n], b * s + to[n]
        pairs.append((a, b))
    return pairs


def neighbour(mesh, parity, flip_y, step_x):
    count = mesh.shape["gx"]

    def move(at):
        if step_x:
            to = at["gx"] + 1 if at["gx"] % 2 == parity else at["gx"] - 1
            if to < 0 or to >= count:
                return None
            at["gx"] = to
        if flip_y:
            at["gy"] = 1 - at["gy"]
        return at

    return permutation(mesh, move)


def call(body, out_shapes, specs, args, out_specs=None, scratch=(), aliases=None):
    return pl.pallas_call(
        body,
        out_shape=out_shapes,
        in_specs=specs,
        out_specs=out_specs if out_specs is not None else [VM] * len(out_shapes),
        scratch_shapes=list(scratch),
        input_output_aliases=aliases or {},
        compiler_params=pltpu.CompilerParams(vmem_limit_bytes=VMEM_LIMIT),
    )(*args)


def shape(*dims):
    return jax.ShapeDtypeStruct(dims, F32)


def message_shapes(geo, first):
    extra = 3 if first else 0
    y = shape(2 * geo.nx + extra * geo.nx // 2, SUB, LANES)
    x = shape(2 * HALO + extra * RADIUS, geo.ny, LANES)
    d = shape(2 * RADIUS // 2, SUB, LANES)
    return [y, x, x, d, d]


def pack_y(geo, fields, my):
    p, _, _ = geo.place()
    nx = geo.nx

    def ybody(x, carry):
        for f, u in enumerate(fields):
            for i in range(2):
                my[f * nx + x, 4 * i : 4 * i + 4, :] = u[x + HALO, pl.ds(4 + i - 2 * p, 4, stride=SUB), :]
        return carry

    lax.fori_loop(0, nx, ybody, 0, unroll=16)

def pack_x(geo, fields, messages):
    p, _, sides = geo.place()
    me, mo, de, do = messages
    nx = geo.nx
    for (right, _), mx, md in zip(sides, (me, mo), (de, do)):
        wide = jnp.where(right, nx, HALO)
        thin = jnp.where(right, nx + HALO - RADIUS, HALO)

        def xbody(i, carry, mx=mx, wide=wide):
            for f, u in enumerate(fields):
                for q in range(geo.srows):
                    mx[f * HALO + i, 4 * q : 4 * q + 4, :] = u[wide + i, pl.ds(2 * p + q, 4, stride=SUB), :]
            return carry

        lax.fori_loop(0, HALO, xbody, 0, unroll=8)
        for i in range(RADIUS):
            for f, u in enumerate(fields):
                rows = u[thin + i, pl.ds(5 - 3 * p, 4, stride=SUB), :]
                md[2 * f + i // 2, 4 * (i % 2) : 4 * (i % 2) + 4, :] = rows


def unpack(geo, fields, extras, messages):
    p, _, sides = geo.place()
    my, me, mo, de, do = messages
    nx = geo.nx

    def ybody(x, carry):
        for f, u in enumerate(fields):
            for i in range(2):
                u[x + HALO, pl.ds(6 + i - 6 * p, 4, stride=SUB), :] = my[f * nx + x, 4 * i : 4 * i + 4, :]
        return carry

    lax.fori_loop(0, nx, ybody, 0, unroll=16)
    if extras:

        def yextra(h, carry):
            for f, u in enumerate(extras):
                for i in range(2):
                    rows = my[2 * nx + f * (nx // 2) + h, 4 * i : 4 * i + 4, :]
                    u[2 * h + i + HALO, pl.ds(6 - 5 * p, 4, stride=SUB), :] = rows
            return carry

        lax.fori_loop(0, nx // 2, yextra, 0, unroll=2)
    for (right, ok), mx, md in zip(sides, (me, mo), (de, do)):

        @pl.when(ok)
        def _(right=right, mx=mx, md=md):
            wide = jnp.where(right, nx + HALO, 0)
            thin = jnp.where(right, nx + HALO, HALO - RADIUS)

            def xbody(i, carry):
                for f, u in enumerate(fields):
                    for q in range(geo.srows):
                        u[wide + i, pl.ds(2 * p + q, 4, stride=SUB), :] = mx[f * HALO + i, 4 * q : 4 * q + 4, :]
                return carry

            lax.fori_loop(0, HALO, xbody, 0, unroll=8)
            for i in range(RADIUS):
                for f, u in enumerate(extras):
                    for q in range(geo.srows):
                        rows = mx[2 * HALO + f * RADIUS + i, 4 * q : 4 * q + 4, :]
                        u[thin + i, pl.ds(2 * p + q, 4, stride=SUB), :] = rows
                for f, u in enumerate(fields):
                    rows = md[2 * f + i // 2, 4 * (i % 2) : 4 * (i % 2) + 4, :]
                    u[thin + i, pl.ds(6 - 5 * p, 4, stride=SUB), :] = rows


def edge_kernel(geo):
    nx = geo.nx

    def body(s0, s1, r0, r1, c0, my, me, mo, de, do, pad, sem):
        p, _, sides = geo.place()
        edge = pl.ds(pl.multiple_of((geo.ny - HALO) * (1 - p), SUB), HALO)
        sources = (s0.at[0], r0.at[0], s1.at[0], r1.at[0], c0)
        copies, along_x = [], []
        for f, src in enumerate(sources):
            to = my.at[f * nx : f * nx + nx] if f < 2 else pad.at[f - 2]
            copies.append(pltpu.make_async_copy(src.at[:, edge, :], to, sem.at[f]))
        for n, ((right, _), mx) in enumerate(zip(sides, (me, mo))):
            for f, src in enumerate(sources):
                planes = HALO if f < 2 else RADIUS
                at = f * HALO if f < 2 else 2 * HALO + (f - 2) * RADIUS
                begin = jnp.where(right, nx - planes, 0)
                along_x.append(
                    pltpu.make_async_copy(src.at[pl.ds(begin, planes)], mx.at[at : at + planes], sem.at[5 * n + 5 + f])
                )
        for copy in copies + along_x:
            copy.start()
        near = pl.ds(4 - 4 * p, 4)
        for f, copy in enumerate(copies):
            copy.wait()
            if f < 2:
                for (right, _), md in zip(sides, (de, do)):
                    begin = f * nx + jnp.where(right, nx - RADIUS, 0)
                    for i in range(RADIUS):
                        md[2 * f + i // 2, 4 * (i % 2) : 4 * (i % 2) + 4, :] = my[begin + i, near, :]
            else:
                for x in range(nx):
                    half = 4 * (x % 2)
                    my[2 * nx + (f - 2) * (nx // 2) + x // 2, half : half + 4, :] = pad[f - 2, x, near, :]
        for copy in along_x:
            copy.wait()

    return body


def load_kernel(geo):
    nx, ny, xe = geo.nx, geo.ny, geo.xe

    def body(s0, s1, r0, r1, c0, us, ur, ps, pr, cc, dw, pad, sem):
        p, _, _ = geo.place()
        inside = pl.ds(pl.multiple_of(SUB * p, SUB), ny)
        sources = (s0.at[0], r0.at[0], s1.at[0], r1.at[0], c0)
        copies = [
            pltpu.make_async_copy(src, pad.at[f, :, inside, :], sem.at[f]) for f, src in enumerate(sources)
        ]
        for copy in copies:
            copy.start()
        outside = pl.ds(pl.multiple_of(ny - ny * p, SUB), SUB)
        targets = (us, ur, ps, pr, cc)
        row = lax.broadcasted_iota(jnp.int32, (LANES, LANES), 0)
        col = lax.broadcasted_iota(jnp.int32, (LANES, LANES), 1)
        gap = jnp.abs(row - col)
        d = jnp.zeros((LANES, LANES), F32)
        for k in range(1, RADIUS + 1):
            d = jnp.where(gap == k, RATIOS[k], d)
        dw[0:LANES, :] = d.astype(jnp.bfloat16)
        dw[LANES : 2 * LANES, :] = d.astype(jnp.bfloat16)
        for i, k in enumerate(FAR):
            at = (2 + i) * LANES
            dw[at : at + LANES, :] = jnp.where(gap == 0, RATIOS[k], 0.0).astype(jnp.bfloat16)
        zero = jnp.zeros((geo.win, LANES), F32)
        for f, u in enumerate(targets):
            for x in range(nx):
                pad[f, x, outside, :] = jnp.zeros((SUB, LANES), F32)
            for x in range(HALO):
                u[x] = zero
                u[nx + HALO + x] = zero
        for f, (u, copy) in enumerate(zip(targets, copies)):
            copy.wait()

            def turn(x, carry, f=f, u=u):
                for j in range(geo.jn):
                    u[x + HALO, SUB * j : SUB * j + SUB, :] = pad[f, x, pl.ds(j, SUB, stride=geo.jn), :]
                return carry

            lax.fori_loop(0, nx, turn, 0, unroll=4)

    return body


def receiver_kernel(geo, nrec):
    rows_all = geo.xe * geo.win
    block = 256

    def body(ri, rc, traces, wavelet, out, wav, table):
        p, g, _ = geo.place()
        x = ri[...] - g * geo.nx + HALO
        w = rc[...] - p * geo.ny + SUB * p
        ok = (x >= 0) & (x < geo.xe) & (w >= 0) & (w < geo.win)
        shift = geo.jn.bit_length() - 1
        row = x * geo.win + (w & (geo.jn - 1)) * SUB + (w >> shift)
        row = jnp.where(ok, row, -1)
        table[...] = jnp.zeros_like(table)
        table[0:STEPS, :] = traces[0] * (1.0 / COEFFS[1])
        wav[...] = jnp.zeros_like(wav)
        wav[0:1, 0:STEPS] = wavelet[...] * (1.0 / COEFFS[1])
        part, left = [], table[...]
        for _ in range(3):
            part.append(left.astype(jnp.bfloat16))
            left = left - part[-1].astype(F32)
        parts = jnp.concatenate(part, axis=1)

        def chunk(i, carry):
            at = i * block + lax.broadcasted_iota(jnp.int32, (block, nrec), 0)
            hot = jnp.where(at == row, 1.0, 0.0).astype(jnp.bfloat16)
            hots = jnp.concatenate([hot, hot, hot], axis=1)
            plane = lax.dot_general(hots, parts, (((1,), (1,)), ((), ())), preferred_element_type=F32)
            planes = block // geo.win
            out[pl.ds(i * planes, planes)] = plane.reshape(planes, geo.win, LANES)
            return carry

        lax.fori_loop(0, rows_all // block, chunk, 0)

    return body


def update_planes(geo, count, pairs, cc, ee, dw, x, moment, gg, corr, fresh):
    jn, span = geo.jn, count * geo.win
    sub = lax.broadcasted_iota(jnp.int32, (SUB, LANES), 0)
    at_depth = lax.broadcasted_iota(jnp.int32, (SUB, LANES), 1) == REC_DEPTH
    first, last = sub == 0, sub == SUB - 1
    parts = []
    for u, _ in pairs:
        rows = u[pl.ds(x - RADIUS, count + 2 * RADIUS)].reshape(span + 2 * RADIUS * geo.win, LANES)
        near_hi = rows.astype(jnp.bfloat16)
        shifted = lambda k: near_hi[(RADIUS + k) * geo.win : (RADIUS + k) * geo.win + span]
        hi = shifted(0)
        lo = (rows[RADIUS * geo.win : RADIUS * geo.win + span] - hi.astype(F32)).astype(jnp.bfloat16)
        parts.append(jnp.concatenate([hi, lo] + [shifted(k) + shifted(-k) for k in FAR], axis=1))
    deep = jnp.dot(jnp.concatenate(parts, axis=0), dw[...], preferred_element_type=F32)
    for i in range(count):
        news = []
        for f, (u, prior) in enumerate(pairs):
            mid = [u[x + i, SUB * j : SUB * j + SUB, :] for j in range(jn)]
            below = [jnp.where(first, 0.0, pltpu.roll(v, 1, 0)) for v in mid]
            above = [jnp.where(last, 0.0, pltpu.roll(v, SUB - 1, 0)) for v in mid]
            line = below + mid + above
            for j in range(jn):
                tile = slice(SUB * j, SUB * j + SUB)
                at = f * span + i * geo.win + SUB * j
                acc = deep[at : at + SUB]
                if f == 1:
                    fed = pltpu.roll(gg[x + i, tile, :], (REC_DEPTH - moment) % LANES, 1)
                    acc = acc + jnp.where(at_depth, fed, 0.0)
                for k in range(1, RADIUS + 1):
                    near = line[jn + j + k] + line[jn + j - k]
                    if k not in FAR:
                        near = (u[x + i + k, tile, :] + u[x + i - k, tile, :]) + near
                    acc = acc + (near if k == 1 else RATIOS[k] * near)
                new = (ee[x + i, tile, :] * mid[j] - prior[x + i, tile, :]) + cc[x + i, tile, :] * acc
                prior[x + i, tile, :] = new
                news.append(new)
        for j in range(jn):
            tile = slice(SUB * j, SUB * j + SUB)
            product = news[j] * news[jn + j]
            if not fresh:
                product = product + corr[x + i - HALO + RADIUS, tile, :]
            corr[x + i - HALO + RADIUS, tile, :] = product


def one_step(geo, moment, us, ur, ps, pr, cc, ee, gg, corr, dw, wav, src, first, count, fresh):
    group_planes = count // TRIPS

    def group(i, carry):
        x = first + i * group_planes
        update_planes(geo, group_planes, ((us, ps), (ur, pr)), cc, ee, dw, x, moment, gg, corr, fresh)
        return carry

    lax.fori_loop(0, TRIPS, group, 0)
    xs, row, ok = src

    @pl.when(ok & (xs >= first) & (xs < first + count))
    def _():
        lane = lax.broadcasted_iota(jnp.int32, (SUB, LANES), 1)
        shot = jnp.where(lane == SRC_DEPTH, pltpu.roll(wav[...], (SRC_DEPTH - moment) % LANES, 1), 0.0)
        add = cc[xs, pl.ds(row, 1), :] * shot[0:1]
        ps[xs, pl.ds(row, 1), :] = ps[xs, pl.ds(row, 1), :] + add
        at = xs - HALO + RADIUS
        corr[at, pl.ds(row, 1), :] = corr[at, pl.ds(row, 1), :] + add * pr[xs, pl.ds(row, 1), :]


def round_kernel(geo, block, last):
    first_round = block == 0

    def body(*refs):
        refs = list(refs)
        take = lambda n: [refs.pop(0) for _ in range(n)]
        take(4)
        if first_round:
            take(1)
        else:
            take(1)
            cc, ee = take(2)
        dw, gg, wav = take(3)
        inputs = take(5)
        sx, sy = take(2)
        us, ur, ps, pr = take(4)
        if first_round:
            cc, ee = take(2)
        (corr,) = take(1)
        outs = [] if last else take(5)
        p, g, _ = geo.place()
        xs = sx[0] - g * geo.nx + HALO
        w = sy[0] - p * geo.ny + SUB * p
        ok = (w >= 0) & (w < geo.win) & (xs >= 0) & (xs < geo.xe)
        shift = geo.jn.bit_length() - 1
        src = (xs, (w & (geo.jn - 1)) * SUB + (w >> shift), ok)
        unpack(geo, (us, ur), (ps, pr, cc) if first_round else (), inputs)
        if first_round:

            def scale(x, carry):
                speed = cc[x]
                ee[x] = 2.0 + (3.0 * COEFFS[0]) * speed
                cc[x] = COEFFS[1] * speed
                return carry

            lax.fori_loop(0, geo.xe, scale, 0, unroll=2)
        common = (cc, ee, gg, corr, dw, wav, src)
        one_step(geo, DEEP * block, us, ur, ps, pr, *common, HALO - RADIUS, geo.nx + 2 * RADIUS, first_round)
        one_step(geo, DEEP * block + 1, ps, pr, us, ur, *common, HALO, geo.nx, False)
        if not last:
            pack_y(geo, (us, ur), outs[0])
            pack_x(geo, (us, ur), outs[1:])

    return body


def corr_kernel(geo, halves):
    part = geo.nx // halves

    def body(corr, mine, other, pad):
        p, _, _ = geo.place()
        q = lax.axis_index("sa")

        def turn(x, carry):
            for j in range(geo.jn):
                pad[x, pl.ds(j, SUB, stride=geo.jn), :] = corr[x + RADIUS, SUB * j : SUB * j + SUB, :]
            return carry

        lax.fori_loop(0, geo.nx, turn, 0, unroll=4)
        inside = pl.ds(pl.multiple_of(SUB * p, SUB), geo.ny)

        def split(x, carry):
            mine[x] = pad[q * part + x, inside, :]
            other[x] = pad[(halves - 1 - q) * part + x, inside, :]
            return carry

        lax.fori_loop(0, part, split, 0, unroll=2)

    return body


def store_kernel(geo):
    def body(us, ur, ps, pr, o0, o1, o2, o3, pad, sem):
        p, _, _ = geo.place()
        inside = pl.ds(pl.multiple_of(SUB * p, SUB), geo.ny)
        copies = []
        for f, (u, o) in enumerate(((us, o0), (ps, o1), (ur, o2), (pr, o3))):

            def turn(x, carry, f=f, u=u):
                for j in range(geo.jn):
                    pad[f, x, pl.ds(j, SUB, stride=geo.jn), :] = u[x + HALO, SUB * j : SUB * j + SUB, :]
                return carry

            lax.fori_loop(0, geo.nx, turn, 0, unroll=4)
            copy = pltpu.make_async_copy(pad.at[f, :, inside, :], o.at[0], sem.at[f])
            copy.start()
            copies.append(copy)
        for copy in copies:
            copy.wait()

    return body


def fast_body(mesh):
    def run(sn, sl, rn, rl, courant, wavelet, traces, si, sc, ri, rc):
        nx, ny, nz = courant.shape
        geo = Geometry(mesh, nx, ny)
        state = shape(geo.xe, geo.win, nz)
        names = mesh.axis_names
        routes = [
            neighbour(mesh, 0, True, False),
            neighbour(mesh, 0, False, True),
            neighbour(mesh, 1, False, True),
            neighbour(mesh, 0, True, True),
            neighbour(mesh, 1, True, True),
        ]
        send = lambda ms: [lax.ppermute(m, names, route) for m, route in zip(ms, routes)]
        given = tuple(pltpu.with_memory_space_constraint(v, pltpu.HBM) for v in (sn, sl, rn, rl, courant))
        first = message_shapes(geo, True)
        messages = send(
            call(
                edge_kernel(geo),
                first,
                [HBM] * 5,
                given,
                scratch=[pltpu.VMEM((3, nx, SUB, nz), F32), pltpu.SemaphoreType.DMA((15,))],
            )
        )
        us, ur, ps, pr, cc, dw = call(
            load_kernel(geo),
            [state] * 5 + [jax.ShapeDtypeStruct(((2 + len(FAR)) * LANES, LANES), jnp.bfloat16)],
            [HBM] * 5,
            given,
            scratch=[pltpu.VMEM((5, nx, geo.win, nz), F32), pltpu.SemaphoreType.DMA((5,))],
        )
        nrec = traces.shape[2]
        gg, wav = call(
            receiver_kernel(geo, nrec),
            [state, shape(SUB, LANES)],
            [VM] * 4,
            (ri, rc, traces, wavelet),
            scratch=[pltpu.VMEM((LANES, nrec), F32)],
        )
        corr_shape = shape(nx + 2 * RADIUS, geo.win, nz)
        corr = ee = None
        blocks = STEPS // DEEP
        for block in range(blocks):
            last = block == blocks - 1
            if block == 0:
                args = [us, ur, ps, pr, cc]
                outs = [state] * 6 + [corr_shape]
                aliases = {i: i for i in range(5)}
            else:
                args = [us, ur, ps, pr, corr, cc, ee]
                outs = [state] * 4 + [corr_shape]
                aliases = {i: i for i in range(5)}
            args = args + [dw, gg, wav] + messages
            outs = call(
                round_kernel(geo, block, last),
                outs + ([] if last else message_shapes(geo, False)),
                [VM] * len(args) + [SM] * 2,
                args + [si, sc],
                aliases=aliases,
            )
            us, ur, ps, pr = outs[:4]
            if block == 0:
                cc, ee, corr = outs[4:7]
            else:
                corr = outs[4]
            if not last:
                messages = send(outs[-5:])
        halves = mesh.shape["sa"]
        part = shape(nx // halves, ny, nz)
        mine, other = call(
            corr_kernel(geo, halves), [part] * 2, [VM], (corr,), scratch=[pltpu.VMEM((nx, geo.win, nz), F32)]
        )
        pairs = [(i, halves - 1 - i) for i in range(halves)]
        image = (mine + lax.ppermute(other, "sa", pairs)) / STEPS
        fields = call(
            store_kernel(geo),
            [shape(1, nx, ny, nz)] * 4,
            [VM] * 4,
            (us, ur, ps, pr),
            out_specs=[HBM] * 4,
            scratch=[pltpu.VMEM((4, nx, geo.win, nz), F32), pltpu.SemaphoreType.DMA((4,))],
        )
        return (*fields, image)

    return run


def padded_2(cells, sides, width):
    for axis, dim in sides:
        count = lax.axis_size(axis)
        ends = count - 1
        head = lax.slice_in_dim(cells, 0, width, axis=dim)
        tail = lax.slice_in_dim(cells, cells.shape[dim] - width, cells.shape[dim], axis=dim)
        cells = jnp.concatenate(
            [
                lax.ppermute(tail, axis, [(i, (i + 1) % count) for i in range(ends)]),
                cells,
                lax.ppermute(head, axis, [((i + 1) % count, i) for i in range(ends)]),
            ],
            axis=dim,
        )
    return cells


def laplace(padded):
    inline_span = padded.shape[0] - 8
    cross_span = padded.shape[1] - 8
    center = padded[4 : 4 + inline_span, 4 : 4 + cross_span]
    depth_span = center.shape[2]
    depth_padded = jnp.pad(center, ((0, 0), (0, 0), (4, 4)))
    summed = 3.0 * COEFFS[0] * center
    for distance in range(1, 5):
        neighbours = (
            padded[4 + distance : 4 + distance + inline_span, 4 : 4 + cross_span]
            + padded[4 - distance : 4 - distance + inline_span, 4 : 4 + cross_span]
        )
        neighbours = (
            neighbours
            + padded[4 : 4 + inline_span, 4 + distance : 4 + distance + cross_span]
            + padded[4 : 4 + inline_span, 4 - distance : 4 - distance + cross_span]
        )
        neighbours = (
            neighbours
            + depth_padded[:, :, 4 + distance : 4 + distance + depth_span]
            + depth_padded[:, :, 4 - distance : 4 - distance + depth_span]
        )
        summed = summed + COEFFS[distance] * neighbours
    return summed


def crop_margin(values, margin_cut):
    if margin_cut == 0:
        return values
    return values[
        margin_cut : values.shape[0] - margin_cut, margin_cut : values.shape[1] - margin_cut
    ]


def general_body(
    source_now,
    source_later,
    receiver_now,
    receiver_later,
    courant,
    wavelet,
    traces,
    source_inline,
    source_crossline,
    receiver_inline,
    receiver_crossline,
):
    inline_count, cross_count, depth_count = courant.shape
    inline_anchor = lax.axis_index("gx") * inline_count
    cross_anchor = lax.axis_index("gy") * cross_count
    inline_extent = inline_count * lax.axis_size("gx")
    cross_extent = cross_count * lax.axis_size("gy")
    depth_axis = jnp.arange(depth_count)
    source_layer = (depth_axis == SRC_DEPTH).astype(jnp.float32)
    receiver_layer = (depth_axis == REC_DEPTH).astype(jnp.float32)
    wavelet_row = wavelet[0]
    records = traces[0]
    source_field = source_now[0]
    source_prior = source_later[0]
    receiver_field = receiver_now[0]
    receiver_prior = receiver_later[0]
    correlation = jnp.zeros(courant.shape, jnp.float32)
    widest = 4 * (GENERAL_BLOCK - 1)
    speed_wide = padded_2(courant, (("gx", 0), ("gy", 1)), widest)
    inline_cells = inline_anchor - widest + jnp.arange(inline_count + 2 * widest)
    cross_cells = cross_anchor - widest + jnp.arange(cross_count + 2 * widest)
    inline_hot = (inline_cells[:, None] == receiver_inline[0][None, :]).astype(jnp.float32)
    cross_hot = (receiver_crossline[0][:, None] == cross_cells[None, :]).astype(jnp.float32)
    receivers = cross_hot.shape[0]
    weighted = (records.T[:, :, None] * cross_hot[:, None, :]).reshape(
        receivers, STEPS * cross_hot.shape[1]
    )
    planes = jnp.dot(inline_hot, weighted, precision=lax.Precision.HIGHEST).reshape(
        inline_hot.shape[0], STEPS, cross_hot.shape[1]
    )
    source_spot = (inline_cells == source_inline[0]).astype(jnp.float32)[:, None] * (
        cross_cells == source_crossline[0]
    ).astype(jnp.float32)[None, :]
    inline_in = ((inline_cells >= 0) & (inline_cells < inline_extent)).astype(jnp.float32)
    cross_in = ((cross_cells >= 0) & (cross_cells < cross_extent)).astype(jnp.float32)
    inside = inline_in[:, None, None] * cross_in[None, :, None]
    planes, source_spot, inside = (planes, source_spot, inside)
    for segment in range(GENERAL_BLOCKS):
        source_wide, receiver_wide = (
            padded_2(source_field, (("gx", 0), ("gy", 1)), 4 * GENERAL_BLOCK),
            padded_2(receiver_field, (("gx", 0), ("gy", 1)), 4 * GENERAL_BLOCK),
        )
        source_back, receiver_back = (
            padded_2(source_prior, (("gx", 0), ("gy", 1)), widest),
            padded_2(receiver_prior, (("gx", 0), ("gy", 1)), widest),
        )
        for substep in range(GENERAL_BLOCK):
            margin = 4 * (GENERAL_BLOCK - 1 - substep)
            offset = widest - margin
            moment = segment * GENERAL_BLOCK + substep
            speed = crop_margin(speed_wide, offset)
            region = crop_margin(inside, offset)
            record_plane = crop_margin(planes[:, moment, :], offset)
            spot_plane = crop_margin(source_spot, offset)
            source_centre = crop_margin(source_wide, 4)
            receiver_centre = crop_margin(receiver_wide, 4)
            source_new = region * (
                2.0 * source_centre
                - source_back
                + speed
                * (
                    laplace(source_wide)
                    + (wavelet_row[moment] * spot_plane)[:, :, None] * source_layer
                )
            )
            receiver_new = region * (
                2.0 * receiver_centre
                - receiver_back
                + speed * (laplace(receiver_wide) + record_plane[:, :, None] * receiver_layer)
            )
            correlation = correlation + crop_margin(source_new, margin) * crop_margin(
                receiver_new, margin
            )
            source_wide, receiver_wide = (source_new, receiver_new)
            if margin > 0:
                source_back = crop_margin(source_centre, 4)
                receiver_back = crop_margin(receiver_centre, 4)
            else:
                source_back = source_centre
                receiver_back = receiver_centre
        source_field, source_prior = (source_wide, source_back)
        receiver_field, receiver_prior = (receiver_wide, receiver_back)
    image_part = lax.psum_scatter(correlation, "sa", scatter_dimension=0, tiled=True) / STEPS
    return (
        source_field[None],
        source_prior[None],
        receiver_field[None],
        receiver_prior[None],
        image_part,
    )


def any_body(mesh):
    fast = fast_body(mesh)

    def run(*args):
        nx, ny, nz = args[4].shape
        fits = mesh.shape["gy"] == 2 and mesh.shape["sa"] == 2 and nz == LANES
        fits = fits and (ny + HALO) == RADIUS * SUB and nx % (2 * HALO) == 0
        return (fast if fits else general_body)(*args)

    return run


def solution(mesh):
    in_specs = (
        P(("groups", "sa"), "gx", "gy", None),
        P(("groups", "sa"), "gx", "gy", None),
        P(("groups", "sa"), "gx", "gy", None),
        P(("groups", "sa"), "gx", "gy", None),
        P("gx", "gy", None),
        P(("groups", "sa"), None),
        P(("groups", "sa"), None, None),
        P(("groups", "sa")),
        P(("groups", "sa")),
        P(("groups", "sa"), None),
        P(("groups", "sa"), None),
    )
    out_specs = (
        P(("groups", "sa"), "gx", "gy", None),
        P(("groups", "sa"), "gx", "gy", None),
        P(("groups", "sa"), "gx", "gy", None),
        P(("groups", "sa"), "gx", "gy", None),
        P(("groups", "gx", "sa"), "gy", None),
    )
    return jax.shard_map(any_body(mesh), mesh=mesh, in_specs=in_specs, out_specs=out_specs, check_vma=False)
```

```python
import itertools

import jax
import jax.numpy as jnp
from jax import lax
from jax.experimental import pallas as pl
from jax.experimental.pallas import tpu as pltpu
from jax.sharding import PartitionSpec as P

SRC_DEPTH = 3
REC_DEPTH = 2
STEPS = 12
COEFFS = (-205.0 / 72.0, 8.0 / 5.0, -1.0 / 5.0, 8.0 / 315.0, -1.0 / 560.0)
RADIUS = 4
LANES = 128
SUB = 8
DEEP = 2
HALO = RADIUS * DEEP
RATIOS = [c / COEFFS[1] for c in COEFFS]
GENERAL_BLOCK = 4
GENERAL_BLOCKS = 3
VMEM_LIMIT = 24 << 20

VM = pl.BlockSpec(memory_space=pltpu.VMEM)
SM = pl.BlockSpec(memory_space=pltpu.SMEM)
HBM = pl.BlockSpec(memory_space=pltpu.HBM)
F32 = jnp.float32


class Geometry:
    def __init__(self, mesh, nx, ny):
        self.mesh = mesh
        self.nx, self.ny = nx, ny
        self.xe = nx + 2 * HALO
        self.win = ny + HALO
        self.jn = self.win // SUB
        self.gx = mesh.shape["gx"]
        self.srows = ny // self.jn

    def place(self):
        p = lax.axis_index("gy")
        g = lax.axis_index("gx")
        odd = g % 2
        even_right = odd == 0
        even_ok = jnp.logical_or(odd == 1, g + 1 < self.gx)
        odd_right = odd == 1
        odd_ok = jnp.logical_or(jnp.logical_and(odd == 1, g + 1 < self.gx), jnp.logical_and(odd == 0, g > 0))
        return p, g, ((even_right, even_ok), (odd_right, odd_ok))


def permutation(mesh, move):
    names = mesh.axis_names
    sizes = [mesh.shape[n] for n in names]
    pairs = []
    for idx in itertools.product(*[range(s) for s in sizes]):
        at = dict(zip(names, idx))
        to = move(dict(at))
        if to is None:
            to = dict(at)
            to["sa"] = (mesh.shape["sa"] - 1) - at["sa"]
        a = b = 0
        for n, s in zip(names, sizes):
            a, b = a * s + at[n], b * s + to[n]
        pairs.append((a, b))
    return pairs


def neighbour(mesh, parity, flip_y, step_x):
    count = mesh.shape["gx"]

    def move(at):
        if step_x:
            to = at["gx"] + 1 if at["gx"] % 2 == parity else at["gx"] - 1
            if to < 0 or to >= count:
                return None
            at["gx"] = to
        if flip_y:
            at["gy"] = 1 - at["gy"]
        return at

    return permutation(mesh, move)


def call(body, out_shapes, specs, args, out_specs=None, scratch=(), aliases=None):
    return pl.pallas_call(
        body,
        out_shape=out_shapes,
        in_specs=specs,
        out_specs=out_specs if out_specs is not None else [VM] * len(out_shapes),
        scratch_shapes=list(scratch),
        input_output_aliases=aliases or {},
        compiler_params=pltpu.CompilerParams(vmem_limit_bytes=VMEM_LIMIT),
    )(*args)


def shape(*dims):
    return jax.ShapeDtypeStruct(dims, F32)


def message_shapes(geo, first):
    extra = 3 if first else 0
    y = shape(2 * geo.nx + extra * geo.nx // 2, SUB, LANES)
    x = shape(2 * HALO + extra * RADIUS, geo.ny, LANES)
    d = shape(2 * RADIUS // 2, SUB, LANES)
    return [y, x, x, d, d]


def pack_y(geo, fields, my):
    p, _, _ = geo.place()
    nx = geo.nx

    def ybody(x, carry):
        for f, u in enumerate(fields):
            for i in range(2):
                my[f * nx + x, 4 * i : 4 * i + 4, :] = u[x + HALO, pl.ds(4 + i - 2 * p, 4, stride=SUB), :]
        return carry

    lax.fori_loop(0, nx, ybody, 0, unroll=16)

def pack_x(geo, fields, messages):
    p, _, sides = geo.place()
    me, mo, de, do = messages
    nx = geo.nx
    for (right, _), mx, md in zip(sides, (me, mo), (de, do)):
        wide = jnp.where(right, nx, HALO)
        thin = jnp.where(right, nx + HALO - RADIUS, HALO)

        def xbody(i, carry, mx=mx, wide=wide):
            for f, u in enumerate(fields):
                for q in range(geo.srows):
                    mx[f * HALO + i, 4 * q : 4 * q + 4, :] = u[wide + i, pl.ds(2 * p + q, 4, stride=SUB), :]
            return carry

        lax.fori_loop(0, HALO, xbody, 0, unroll=8)
        for i in range(RADIUS):
            for f, u in enumerate(fields):
                rows = u[thin + i, pl.ds(5 - 3 * p, 4, stride=SUB), :]
                md[2 * f + i // 2, 4 * (i % 2) : 4 * (i % 2) + 4, :] = rows


def unpack(geo, fields, extras, messages):
    p, _, sides = geo.place()
    my, me, mo, de, do = messages
    nx = geo.nx

    def ybody(x, carry):
        for f, u in enumerate(fields):
            for i in range(2):
                u[x + HALO, pl.ds(6 + i - 6 * p, 4, stride=SUB), :] = my[f * nx + x, 4 * i : 4 * i + 4, :]
        return carry

    lax.fori_loop(0, nx, ybody, 0, unroll=16)
    if extras:

        def yextra(h, carry):
            for f, u in enumerate(extras):
                for i in range(2):
                    rows = my[2 * nx + f * (nx // 2) + h, 4 * i : 4 * i + 4, :]
                    u[2 * h + i + HALO, pl.ds(6 - 5 * p, 4, stride=SUB), :] = rows
            return carry

        lax.fori_loop(0, nx // 2, yextra, 0, unroll=2)
    for (right, ok), mx, md in zip(sides, (me, mo), (de, do)):

        @pl.when(ok)
        def _(right=right, mx=mx, md=md):
            wide = jnp.where(right, nx + HALO, 0)
            thin = jnp.where(right, nx + HALO, HALO - RADIUS)

            def xbody(i, carry):
                for f, u in enumerate(fields):
                    for q in range(geo.srows):
                        u[wide + i, pl.ds(2 * p + q, 4, stride=SUB), :] = mx[f * HALO + i, 4 * q : 4 * q + 4, :]
                return carry

            lax.fori_loop(0, HALO, xbody, 0, unroll=8)
            for i in range(RADIUS):
                for f, u in enumerate(extras):
                    for q in range(geo.srows):
                        rows = mx[2 * HALO + f * RADIUS + i, 4 * q : 4 * q + 4, :]
                        u[thin + i, pl.ds(2 * p + q, 4, stride=SUB), :] = rows
                for f, u in enumerate(fields):
                    rows = md[2 * f + i // 2, 4 * (i % 2) : 4 * (i % 2) + 4, :]
                    u[thin + i, pl.ds(6 - 5 * p, 4, stride=SUB), :] = rows


def edge_kernel(geo):
    nx = geo.nx

    def body(s0, s1, r0, r1, c0, my, me, mo, de, do, pad, sem):
        p, _, sides = geo.place()
        edge = pl.ds(pl.multiple_of((geo.ny - HALO) * (1 - p), SUB), HALO)
        sources = (s0.at[0], r0.at[0], s1.at[0], r1.at[0], c0)
        copies, along_x = [], []
        for f, src in enumerate(sources):
            to = my.at[f * nx : f * nx + nx] if f < 2 else pad.at[f - 2]
            copies.append(pltpu.make_async_copy(src.at[:, edge, :], to, sem.at[f]))
        for n, ((right, _), mx) in enumerate(zip(sides, (me, mo))):
            for f, src in enumerate(sources):
                planes = HALO if f < 2 else RADIUS
                at = f * HALO if f < 2 else 2 * HALO + (f - 2) * RADIUS
                begin = jnp.where(right, nx - planes, 0)
                along_x.append(
                    pltpu.make_async_copy(src.at[pl.ds(begin, planes)], mx.at[at : at + planes], sem.at[5 * n + 5 + f])
                )
        for copy in copies + along_x:
            copy.start()
        near = pl.ds(4 - 4 * p, 4)
        for f, copy in enumerate(copies):
            copy.wait()
            if f < 2:
                for (right, _), md in zip(sides, (de, do)):
                    begin = f * nx + jnp.where(right, nx - RADIUS, 0)
                    for i in range(RADIUS):
                        md[2 * f + i // 2, 4 * (i % 2) : 4 * (i % 2) + 4, :] = my[begin + i, near, :]
            else:
                for x in range(nx):
                    half = 4 * (x % 2)
                    my[2 * nx + (f - 2) * (nx // 2) + x // 2, half : half + 4, :] = pad[f - 2, x, near, :]
        for copy in along_x:
            copy.wait()

    return body


def load_kernel(geo):
    nx, ny, xe = geo.nx, geo.ny, geo.xe

    def body(s0, s1, r0, r1, c0, us, ur, ps, pr, cc, dw, pad, sem):
        p, _, _ = geo.place()
        inside = pl.ds(pl.multiple_of(SUB * p, SUB), ny)
        sources = (s0.at[0], r0.at[0], s1.at[0], r1.at[0], c0)
        copies = [
            pltpu.make_async_copy(src, pad.at[f, :, inside, :], sem.at[f]) for f, src in enumerate(sources)
        ]
        for copy in copies:
            copy.start()
        outside = pl.ds(pl.multiple_of(ny - ny * p, SUB), SUB)
        targets = (us, ur, ps, pr, cc)
        row = lax.broadcasted_iota(jnp.int32, (LANES, LANES), 0)
        col = lax.broadcasted_iota(jnp.int32, (LANES, LANES), 1)
        gap = jnp.abs(row - col)
        d = jnp.zeros((LANES, LANES), F32)
        for k in range(1, RADIUS + 1):
            d = jnp.where(gap == k, RATIOS[k], d)
        dw[0:LANES, :] = d.astype(jnp.bfloat16)
        dw[LANES : 2 * LANES, :] = d.astype(jnp.bfloat16)
        zero = jnp.zeros((geo.win, LANES), F32)
        for f, u in enumerate(targets):
            for x in range(nx):
                pad[f, x, outside, :] = jnp.zeros((SUB, LANES), F32)
            for x in range(HALO):
                u[x] = zero
                u[nx + HALO + x] = zero
        for f, (u, copy) in enumerate(zip(targets, copies)):
            copy.wait()

            def turn(x, carry, f=f, u=u):
                for j in range(geo.jn):
                    u[x + HALO, SUB * j : SUB * j + SUB, :] = pad[f, x, pl.ds(j, SUB, stride=geo.jn), :]
                return carry

            lax.fori_loop(0, nx, turn, 0, unroll=4)

    return body


def receiver_kernel(geo, nrec):
    rows_all = geo.xe * geo.win
    block = 256

    def body(ri, rc, traces, wavelet, out, wav, table):
        p, g, _ = geo.place()
        x = ri[...] - g * geo.nx + HALO
        w = rc[...] - p * geo.ny + SUB * p
        ok = (x >= 0) & (x < geo.xe) & (w >= 0) & (w < geo.win)
        shift = geo.jn.bit_length() - 1
        row = x * geo.win + (w & (geo.jn - 1)) * SUB + (w >> shift)
        row = jnp.where(ok, row, -1)
        table[...] = jnp.zeros_like(table)
        table[0:STEPS, :] = traces[0] * (1.0 / COEFFS[1])
        wav[...] = jnp.zeros_like(wav)
        wav[0:1, 0:STEPS] = wavelet[...] * (1.0 / COEFFS[1])
        part, left = [], table[...]
        for _ in range(3):
            part.append(left.astype(jnp.bfloat16))
            left = left - part[-1].astype(F32)
        parts = jnp.concatenate(part, axis=1)

        def chunk(i, carry):
            at = i * block + lax.broadcasted_iota(jnp.int32, (block, nrec), 0)
            hot = jnp.where(at == row, 1.0, 0.0).astype(jnp.bfloat16)
            hots = jnp.concatenate([hot, hot, hot], axis=1)
            plane = lax.dot_general(hots, parts, (((1,), (1,)), ((), ())), preferred_element_type=F32)
            planes = block // geo.win
            out[pl.ds(i * planes, planes)] = plane.reshape(planes, geo.win, LANES)
            return carry

        lax.fori_loop(0, rows_all // block, chunk, 0)

    return body


def update_planes(geo, count, pairs, cc, ee, dw, x, moment, gg, corr, fresh, masked):
    jn, span = geo.jn, count * geo.win
    sub = lax.broadcasted_iota(jnp.int32, (SUB, LANES), 0)
    at_depth = lax.broadcasted_iota(jnp.int32, (SUB, LANES), 1) == REC_DEPTH
    first, last = sub == 0, sub == SUB - 1
    rows = jnp.concatenate([u[pl.ds(x, count)].reshape(span, LANES) for u, _ in pairs], axis=0)
    hi = rows.astype(jnp.bfloat16)
    lo = (rows - hi.astype(F32)).astype(jnp.bfloat16)
    deep = jnp.dot(jnp.concatenate([hi, lo], axis=1), dw[...], preferred_element_type=F32)
    for i in range(count):
        news = []
        for f, (u, prior) in enumerate(pairs):
            mid = [u[x + i, SUB * j : SUB * j + SUB, :] for j in range(jn)]
            below = [pltpu.roll(v, 1, 0) for v in mid]
            above = [pltpu.roll(v, SUB - 1, 0) for v in mid]
            if masked:
                below = [jnp.where(first, 0.0, v) for v in below]
                above = [jnp.where(last, 0.0, v) for v in above]
            line = below + mid + above
            for j in range(jn):
                tile = slice(SUB * j, SUB * j + SUB)
                at = f * span + i * geo.win + SUB * j
                acc = deep[at : at + SUB]
                if f == 1:
                    fed = pltpu.roll(gg[x + i, tile, :], (REC_DEPTH - moment) % LANES, 1)
                    acc = acc + jnp.where(at_depth, fed, 0.0)
                for k in range(1, RADIUS + 1):
                    near = (u[x + i + k, tile, :] + u[x + i - k, tile, :]) + (line[jn + j + k] + line[jn + j - k])
                    acc = acc + (near if k == 1 else RATIOS[k] * near)
                new = (ee[x + i, tile, :] * mid[j] - prior[x + i, tile, :]) + cc[x + i, tile, :] * acc
                prior[x + i, tile, :] = new
                news.append(new)
        at = x + i - HALO
        if 0 <= at < geo.nx:
            for j in range(jn):
                tile = slice(SUB * j, SUB * j + SUB)
                product = news[j] * news[jn + j]
                if not fresh:
                    product = product + corr[at, tile, :]
                corr[at, tile, :] = product


def one_step(geo, moment, us, ur, ps, pr, cc, ee, gg, corr, dw, wav, src, first, count, fresh, masked):
    update_planes(geo, count, ((us, ps), (ur, pr)), cc, ee, dw, first, moment, gg, corr, fresh, masked)
    xs, row, ok = src

    @pl.when(ok & (xs >= first) & (xs < first + count))
    def _():
        lane = lax.broadcasted_iota(jnp.int32, (SUB, LANES), 1)
        shot = jnp.where(lane == SRC_DEPTH, pltpu.roll(wav[...], (SRC_DEPTH - moment) % LANES, 1), 0.0)
        add = cc[xs, pl.ds(row, 1), :] * shot[0:1]
        ps[xs, pl.ds(row, 1), :] = ps[xs, pl.ds(row, 1), :] + add

        @pl.when((xs >= HALO) & (xs < geo.nx + HALO))
        def _():
            at = xs - HALO
            corr[at, pl.ds(row, 1), :] = corr[at, pl.ds(row, 1), :] + add * pr[xs, pl.ds(row, 1), :]


def round_kernel(geo, block, last):
    first_round = block == 0

    def body(*refs):
        refs = list(refs)
        take = lambda n: [refs.pop(0) for _ in range(n)]
        take(4)
        if first_round:
            take(1)
        else:
            take(1)
            cc, ee = take(2)
        dw, gg, wav = take(3)
        inputs = take(5)
        sx, sy = take(2)
        us, ur, ps, pr = take(4)
        if first_round:
            cc, ee = take(2)
        (corr,) = take(1)
        outs = [] if last else take(5)
        p, g, _ = geo.place()
        xs = sx[0] - g * geo.nx + HALO
        w = sy[0] - p * geo.ny + SUB * p
        ok = (w >= 0) & (w < geo.win) & (xs >= 0) & (xs < geo.xe)
        shift = geo.jn.bit_length() - 1
        src = (xs, (w & (geo.jn - 1)) * SUB + (w >> shift), ok)
        unpack(geo, (us, ur), (ps, pr, cc) if first_round else (), inputs)
        if first_round:

            sub = lax.broadcasted_iota(jnp.int32, (geo.win, LANES), 0) & (SUB - 1)
            outer = sub == (SUB - 1) * (1 - p)

            def scale(x, carry):
                speed = cc[x]
                ee[x] = jnp.where(outer, 0.0, 2.0 + (3.0 * COEFFS[0]) * speed)
                cc[x] = COEFFS[1] * speed
                return carry

            lax.fori_loop(0, geo.xe, scale, 0, unroll=2)
        common = (cc, ee, gg, corr, dw, wav, src)
        one_step(geo, DEEP * block, us, ur, ps, pr, *common, HALO - RADIUS, geo.nx + 2 * RADIUS, first_round, True)
        one_step(geo, DEEP * block + 1, ps, pr, us, ur, *common, HALO, geo.nx, False, False)
        if not last:
            pack_y(geo, (us, ur), outs[0])
            pack_x(geo, (us, ur), outs[1:])

    return body


def corr_kernel(geo, halves):
    part = geo.nx // halves

    def body(corr, mine, other, pad):
        p, _, _ = geo.place()
        q = lax.axis_index("sa")

        def turn(x, carry):
            for j in range(geo.jn):
                pad[x, pl.ds(j, SUB, stride=geo.jn), :] = corr[x, SUB * j : SUB * j + SUB, :]
            return carry

        lax.fori_loop(0, geo.nx, turn, 0, unroll=4)
        inside = pl.ds(pl.multiple_of(SUB * p, SUB), geo.ny)

        def split(x, carry):
            mine[x] = pad[q * part + x, inside, :]
            other[x] = pad[(halves - 1 - q) * part + x, inside, :]
            return carry

        lax.fori_loop(0, part, split, 0, unroll=2)

    return body


def store_kernel(geo):
    def body(us, ur, ps, pr, o0, o1, o2, o3, pad, sem):
        p, _, _ = geo.place()
        inside = pl.ds(pl.multiple_of(SUB * p, SUB), geo.ny)
        copies = []
        for f, (u, o) in enumerate(((us, o0), (ps, o1), (ur, o2), (pr, o3))):

            def turn(x, carry, f=f, u=u):
                for j in range(geo.jn):
                    pad[f, x, pl.ds(j, SUB, stride=geo.jn), :] = u[x + HALO, SUB * j : SUB * j + SUB, :]
                return carry

            lax.fori_loop(0, geo.nx, turn, 0, unroll=4)
            copy = pltpu.make_async_copy(pad.at[f, :, inside, :], o.at[0], sem.at[f])
            copy.start()
            copies.append(copy)
        for copy in copies:
            copy.wait()

    return body


def fast_body(mesh):
    def run(sn, sl, rn, rl, courant, wavelet, traces, si, sc, ri, rc):
        nx, ny, nz = courant.shape
        geo = Geometry(mesh, nx, ny)
        state = shape(geo.xe, geo.win, nz)
        names = mesh.axis_names
        routes = [
            neighbour(mesh, 0, True, False),
            neighbour(mesh, 0, False, True),
            neighbour(mesh, 1, False, True),
            neighbour(mesh, 0, True, True),
            neighbour(mesh, 1, True, True),
        ]
        send = lambda ms: [lax.ppermute(m, names, route) for m, route in zip(ms, routes)]
        given = tuple(pltpu.with_memory_space_constraint(v, pltpu.HBM) for v in (sn, sl, rn, rl, courant))
        first = message_shapes(geo, True)
        messages = send(
            call(
                edge_kernel(geo),
                first,
                [HBM] * 5,
                given,
                scratch=[pltpu.VMEM((3, nx, SUB, nz), F32), pltpu.SemaphoreType.DMA((15,))],
            )
        )
        us, ur, ps, pr, cc, dw = call(
            load_kernel(geo),
            [state] * 5 + [jax.ShapeDtypeStruct((2 * LANES, LANES), jnp.bfloat16)],
            [HBM] * 5,
            given,
            scratch=[pltpu.VMEM((5, nx, geo.win, nz), F32), pltpu.SemaphoreType.DMA((5,))],
        )
        nrec = traces.shape[2]
        gg, wav = call(
            receiver_kernel(geo, nrec),
            [state, shape(SUB, LANES)],
            [VM] * 4,
            (ri, rc, traces, wavelet),
            scratch=[pltpu.VMEM((LANES, nrec), F32)],
        )
        corr_shape = shape(nx, geo.win, nz)
        corr = ee = None
        blocks = STEPS // DEEP
        for block in range(blocks):
            last = block == blocks - 1
            if block == 0:
                args = [us, ur, ps, pr, cc]
                outs = [state] * 6 + [corr_shape]
                aliases = {i: i for i in range(5)}
            else:
                args = [us, ur, ps, pr, corr, cc, ee]
                outs = [state] * 4 + [corr_shape]
                aliases = {i: i for i in range(5)}
            args = args + [dw, gg, wav] + messages
            outs = call(
                round_kernel(geo, block, last),
                outs + ([] if last else message_shapes(geo, False)),
                [VM] * len(args) + [SM] * 2,
                args + [si, sc],
                aliases=aliases,
            )
            us, ur, ps, pr = outs[:4]
            if block == 0:
                cc, ee, corr = outs[4:7]
            else:
                corr = outs[4]
            if not last:
                messages = send(outs[-5:])
        halves = mesh.shape["sa"]
        part = shape(nx // halves, ny, nz)
        mine, other = call(
            corr_kernel(geo, halves), [part] * 2, [VM], (corr,), scratch=[pltpu.VMEM((nx, geo.win, nz), F32)]
        )
        pairs = [(i, halves - 1 - i) for i in range(halves)]
        image = (mine + lax.ppermute(other, "sa", pairs)) / STEPS
        fields = call(
            store_kernel(geo),
            [shape(1, nx, ny, nz)] * 4,
            [VM] * 4,
            (us, ur, ps, pr),
            out_specs=[HBM] * 4,
            scratch=[pltpu.VMEM((4, nx, geo.win, nz), F32), pltpu.SemaphoreType.DMA((4,))],
        )
        return (*fields, image)

    return run


def padded_2(cells, sides, width):
    for axis, dim in sides:
        count = lax.axis_size(axis)
        ends = count - 1
        head = lax.slice_in_dim(cells, 0, width, axis=dim)
        tail = lax.slice_in_dim(cells, cells.shape[dim] - width, cells.shape[dim], axis=dim)
        cells = jnp.concatenate(
            [
                lax.ppermute(tail, axis, [(i, (i + 1) % count) for i in range(ends)]),
                cells,
                lax.ppermute(head, axis, [((i + 1) % count, i) for i in range(ends)]),
            ],
            axis=dim,
        )
    return cells


def laplace(padded):
    inline_span = padded.shape[0] - 8
    cross_span = padded.shape[1] - 8
    center = padded[4 : 4 + inline_span, 4 : 4 + cross_span]
    depth_span = center.shape[2]
    depth_padded = jnp.pad(center, ((0, 0), (0, 0), (4, 4)))
    summed = 3.0 * COEFFS[0] * center
    for distance in range(1, 5):
        neighbours = (
            padded[4 + distance : 4 + distance + inline_span, 4 : 4 + cross_span]
            + padded[4 - distance : 4 - distance + inline_span, 4 : 4 + cross_span]
        )
        neighbours = (
            neighbours
            + padded[4 : 4 + inline_span, 4 + distance : 4 + distance + cross_span]
            + padded[4 : 4 + inline_span, 4 - distance : 4 - distance + cross_span]
        )
        neighbours = (
            neighbours
            + depth_padded[:, :, 4 + distance : 4 + distance + depth_span]
            + depth_padded[:, :, 4 - distance : 4 - distance + depth_span]
        )
        summed = summed + COEFFS[distance] * neighbours
    return summed


def crop_margin(values, margin_cut):
    if margin_cut == 0:
        return values
    return values[
        margin_cut : values.shape[0] - margin_cut, margin_cut : values.shape[1] - margin_cut
    ]


def general_body(
    source_now,
    source_later,
    receiver_now,
    receiver_later,
    courant,
    wavelet,
    traces,
    source_inline,
    source_crossline,
    receiver_inline,
    receiver_crossline,
):
    inline_count, cross_count, depth_count = courant.shape
    inline_anchor = lax.axis_index("gx") * inline_count
    cross_anchor = lax.axis_index("gy") * cross_count
    inline_extent = inline_count * lax.axis_size("gx")
    cross_extent = cross_count * lax.axis_size("gy")
    depth_axis = jnp.arange(depth_count)
    source_layer = (depth_axis == SRC_DEPTH).astype(jnp.float32)
    receiver_layer = (depth_axis == REC_DEPTH).astype(jnp.float32)
    wavelet_row = wavelet[0]
    records = traces[0]
    source_field = source_now[0]
    source_prior = source_later[0]
    receiver_field = receiver_now[0]
    receiver_prior = receiver_later[0]
    correlation = jnp.zeros(courant.shape, jnp.float32)
    widest = 4 * (GENERAL_BLOCK - 1)
    speed_wide = padded_2(courant, (("gx", 0), ("gy", 1)), widest)
    inline_cells = inline_anchor - widest + jnp.arange(inline_count + 2 * widest)
    cross_cells = cross_anchor - widest + jnp.arange(cross_count + 2 * widest)
    inline_hot = (inline_cells[:, None] == receiver_inline[0][None, :]).astype(jnp.float32)
    cross_hot = (receiver_crossline[0][:, None] == cross_cells[None, :]).astype(jnp.float32)
    receivers = cross_hot.shape[0]
    weighted = (records.T[:, :, None] * cross_hot[:, None, :]).reshape(
        receivers, STEPS * cross_hot.shape[1]
    )
    planes = jnp.dot(inline_hot, weighted, precision=lax.Precision.HIGHEST).reshape(
        inline_hot.shape[0], STEPS, cross_hot.shape[1]
    )
    source_spot = (inline_cells == source_inline[0]).astype(jnp.float32)[:, None] * (
        cross_cells == source_crossline[0]
    ).astype(jnp.float32)[None, :]
    inline_in = ((inline_cells >= 0) & (inline_cells < inline_extent)).astype(jnp.float32)
    cross_in = ((cross_cells >= 0) & (cross_cells < cross_extent)).astype(jnp.float32)
    inside = inline_in[:, None, None] * cross_in[None, :, None]
    planes, source_spot, inside = (planes, source_spot, inside)
    for segment in range(GENERAL_BLOCKS):
        source_wide, receiver_wide = (
            padded_2(source_field, (("gx", 0), ("gy", 1)), 4 * GENERAL_BLOCK),
            padded_2(receiver_field, (("gx", 0), ("gy", 1)), 4 * GENERAL_BLOCK),
        )
        source_back, receiver_back = (
            padded_2(source_prior, (("gx", 0), ("gy", 1)), widest),
            padded_2(receiver_prior, (("gx", 0), ("gy", 1)), widest),
        )
        for substep in range(GENERAL_BLOCK):
            margin = 4 * (GENERAL_BLOCK - 1 - substep)
            offset = widest - margin
            moment = segment * GENERAL_BLOCK + substep
            speed = crop_margin(speed_wide, offset)
            region = crop_margin(inside, offset)
            record_plane = crop_margin(planes[:, moment, :], offset)
            spot_plane = crop_margin(source_spot, offset)
            source_centre = crop_margin(source_wide, 4)
            receiver_centre = crop_margin(receiver_wide, 4)
            source_new = region * (
                2.0 * source_centre
                - source_back
                + speed
                * (
                    laplace(source_wide)
                    + (wavelet_row[moment] * spot_plane)[:, :, None] * source_layer
                )
            )
            receiver_new = region * (
                2.0 * receiver_centre
                - receiver_back
                + speed * (laplace(receiver_wide) + record_plane[:, :, None] * receiver_layer)
            )
            correlation = correlation + crop_margin(source_new, margin) * crop_margin(
                receiver_new, margin
            )
            source_wide, receiver_wide = (source_new, receiver_new)
            if margin > 0:
                source_back = crop_margin(source_centre, 4)
                receiver_back = crop_margin(receiver_centre, 4)
            else:
                source_back = source_centre
                receiver_back = receiver_centre
        source_field, source_prior = (source_wide, source_back)
        receiver_field, receiver_prior = (receiver_wide, receiver_back)
    image_part = lax.psum_scatter(correlation, "sa", scatter_dimension=0, tiled=True) / STEPS
    return (
        source_field[None],
        source_prior[None],
        receiver_field[None],
        receiver_prior[None],
        image_part,
    )


def any_body(mesh):
    fast = fast_body(mesh)

    def run(*args):
        nx, ny, nz = args[4].shape
        fits = mesh.shape["gy"] == 2 and mesh.shape["sa"] == 2 and nz == LANES
        fits = fits and (ny + HALO) == RADIUS * SUB and nx % (2 * HALO) == 0
        return (fast if fits else general_body)(*args)

    return run


def solution(mesh):
    in_specs = (
        P(("groups", "sa"), "gx", "gy", None),
        P(("groups", "sa"), "gx", "gy", None),
        P(("groups", "sa"), "gx", "gy", None),
        P(("groups", "sa"), "gx", "gy", None),
        P("gx", "gy", None),
        P(("groups", "sa"), None),
        P(("groups", "sa"), None, None),
        P(("groups", "sa")),
        P(("groups", "sa")),
        P(("groups", "sa"), None),
        P(("groups", "sa"), None),
    )
    out_specs = (
        P(("groups", "sa"), "gx", "gy", None),
        P(("groups", "sa"), "gx", "gy", None),
        P(("groups", "sa"), "gx", "gy", None),
        P(("groups", "sa"), "gx", "gy", None),
        P(("groups", "gx", "sa"), "gy", None),
    )
    return jax.shard_map(any_body(mesh), mesh=mesh, in_specs=in_specs, out_specs=out_specs, check_vma=False)
```
